512 devices in a mesh: group: 16 (over z, core), dom: 32 (over y, x).
Axes of the slice: x: 4, y: 8, z: 8, core: 2. Of those that a mesh axis runs over, the one named last changes fastest.
Arguments:
- adjoint: float32 [6, 524288], P(None, ('group', 'dom')), may hold values from -4 to 4
- gradient: float32 [6, 524288], P(None, ('group', 'dom')), may hold values from -6 to 6
- precond: float32 [6, 524288], P(None, ('group', 'dom')), may hold values from 0.3 to 1
- band: bfloat16 [5, 6, 6, 524288], P(None, None, None, ('group', 'dom')), may hold values from -0.75 to 0.75
- face_jac: bfloat16 [262144, 768], P(('group', 'dom')), may hold values from -2.5 to 2.5
- face_cell: int32 [262144], P(('group', 'dom')), may hold values from 0 to 32767, as said below
- face_box: int32 [262144, 1], P(('group', 'dom')), may hold values from 0 to 31; in each aligned block of 512 rows (0 to 511, 512 to 1023, ...) at most 64 rows name the same one
Outputs:
- adjoint_out: float32 [6, 524288], P(None, ('group', 'dom'))
- box_sens: float32 [512, 128], P(('group', 'dom'))
The draws below stay inside these ranges and needn't reach their ends.
Inputs may be any that keep to these rules, and one draw needn't show every extreme that they name: `face_box`: within the rows of one device no box is named by more than 64 faces, a bound that some block reaches. `face_cell`: within the faces of one device no partition of 1024 cells (cells p * 1024 to (p + 1) * 1024 - 1) is read by more than 64 faces, and some partition by exactly 64.
All inputs are finite; a program needn't handle non-finite values.
Results may differ from the reference program's by a relative error of at most 0.0003.
Values sent between devices are 32-bit elements; how exact they have to be, the bound alone decides.
A program may use at most 64 MiB of HBM per device.

```python
import math
import jax
import jax.numpy as jnp
import numpy as np
from jax import lax

NVAR = 6
SENS = 128
BAND = 5
SWEEPS = 3
CELL_DEV = 1024
FACE_DEV = 512
CAP = 64
CELLS = 524288
FACES = 262144
BOXES = 512
N_DOM = 32


def draw_face_cell(key, part):
    slot_total = N_DOM * CAP

    def one_block(block_key):
        key_perm, key_owner, key_order, key_cell = jax.random.split(block_key, 4)
        scores = jax.random.permutation(key_perm, slot_total).astype(jnp.int32)
        heavy_owner = jax.random.randint(key_owner, (), 0, N_DOM, dtype=jnp.int32)
        owner_of = jnp.arange(slot_total, dtype=jnp.int32) // CAP
        scores = scores + jnp.where(owner_of == heavy_owner, slot_total, 0).astype(jnp.int32)
        top_values, picked = lax.top_k(scores, FACE_DEV)
        picked = jax.random.permutation(key_order, picked.astype(jnp.int32))
        offset = jax.random.randint(key_cell, (FACE_DEV,), 0, CELL_DEV, dtype=jnp.int32)
        return (picked // CAP * CELL_DEV + offset).astype(jnp.int32)
    block_keys = jax.random.split(key, FACES // FACE_DEV)
    return jax.vmap(one_block)(block_keys).reshape(FACES).astype(jnp.int32)


def level_of(own_key, shape, pieces, low, largest):
    gain, own = 1.0, jax.random.fold_in(own_key, 6)
    for position, blocks in pieces:
        heights = jnp.exp(jax.random.uniform(jax.random.fold_in(own, position), (blocks,), jnp.float32, low / len(pieces), largest / len(pieces)))
        gain = gain * jnp.repeat(heights, shape[position] // blocks).reshape([-1 if axis == position else 1 for axis in range(len(shape))])
    return gain


def deal_out(own_key, own, number, rows, number_of, top, limit, skew):
    ranking = jax.random.permutation(own_key, number_of)
    heavy_load, usual = portions_of(number_of, rows * top, limit, skew, True), portions_of(number_of, rows * top, limit, skew, False)
    places = jnp.arange(number_of)

    def named(sizes, rotation):
        used = int((sizes > 0).sum())
        fixed = max(1, used // 4)
        moved = fixed + (places - fixed + rotation * (used - fixed)) % max(1, number_of - fixed)
        return jnp.zeros((number_of,), jnp.int32).at[ranking[jnp.where(places < fixed, places, moved)]].set(jnp.asarray(sizes, jnp.int32))

    sizes = jnp.where(number % 4 == 0, named(heavy_load, number // 4), named(usual, number - number // 4 - 1))
    mixed = jax.random.permutation(jax.random.fold_in(own, 3), number_of)
    source_of, taker = mixed[0:number_of // 2 * 2:2], mixed[1:number_of // 2 * 2:2]
    slack = jnp.minimum(sizes[source_of] - 1, limit - sizes[taker]) // 2
    slack = jnp.where((source_of == ranking[0]) | (taker == ranking[0]) | (sizes[taker] == 0), 0, jnp.maximum(slack, 0))
    moved = jax.random.randint(jax.random.fold_in(own, 4), (number_of // 2,), 0, 1 << 20) % (slack + 1)
    sizes = sizes.at[source_of].add(-moved).at[taker].add(moved)
    members = jnp.searchsorted(jnp.cumsum(sizes), jnp.arange(rows * top), side="right").astype(jnp.int32)
    listing = members.reshape(top, rows).T
    listing = listing[jax.random.permutation(jax.random.fold_in(own, 1), rows)]
    rotation = jax.random.randint(jax.random.fold_in(own, 2), (rows, 1), 0, top)
    return jnp.take_along_axis(listing, (jnp.arange(top)[None, :] + rotation) % top, axis=1)


def portions_of(count, total, reach, skew, full):
    weights = [(1 << 20) // math.isqrt(standing ** skew) + 1 for standing in range(1, count + 1)]
    largest = reach if full else min(reach, max(-(-total // count), total * weights[0] // sum(weights)))
    least = 1 if total - largest >= count - 1 else 0
    given, rest = [largest] + [least] * (count - 1), total - largest - least * (count - 1)
    while rest > 0:
        free = [i for i in range(1, count) if given[i] < largest] or [i for i in range(1, count) if given[i] < reach]
        whole, budget = sum([weights[i] for i in free]), rest
        for i in free:
            addition = min(reach - given[i], max(1, budget * weights[i] // whole), rest)
            given[i] = given[i] + addition
            rest = rest - addition
    return np.array(given)


def centred(key, extent, deviation, limit, pieces=(), kind=jnp.bfloat16):
    drawn = jax.random.normal(key, extent, jnp.float32) * deviation
    if len(pieces) > 0:
        drawn = level_of(key, extent, pieces, -0.22, 0.18) * drawn
    return jnp.clip(drawn, min=-limit, max=limit).astype(kind)


def setup_inputs(seed: int = 0) -> dict:
    keys = jax.random.split(jax.random.key(seed), 8)
    adjoint = centred(keys[0], (NVAR, CELLS), 0.5, 4.0, ((1, 512),), jnp.float32)
    gradient = centred(keys[1], (NVAR, CELLS), 1.0, 6.0, ((1, 512),), jnp.float32)
    precond = jnp.clip(jnp.exp(math.log(1.0) - 1.2039728 * jax.random.uniform(keys[2], (NVAR, CELLS), jnp.float32) ** level_of(keys[2], (NVAR, CELLS), ((1, 512),), -0.2, 0.2)), 0.3, 1.0)
    band = centred(keys[3], (BAND, NVAR, NVAR, CELLS), 60 ** -0.5, 0.75, ((3, 512),))
    face_jac = centred(keys[4], (FACES, NVAR * SENS), NVAR ** -0.5, 2.5, ((0, 512),))
    face_cell = draw_face_cell(jax.random.fold_in(keys[7], 71), 0)
    face_box_keys = jax.random.split(jax.random.fold_in(keys[6], 1), FACES // FACE_DEV)
    face_box_turns = jax.random.permutation(jax.random.fold_in(keys[6], 3), FACES // FACE_DEV)
    face_box = jax.vmap(lambda own, number: deal_out(jax.random.fold_in(keys[6], 2), own, number, FACE_DEV, N_DOM, 1, CAP, 2))(face_box_keys, face_box_turns).reshape((FACES, 1))
    return {"adjoint": adjoint, "gradient": gradient, "precond": precond, "band": band, "face_jac": face_jac, "face_cell": face_cell, "face_box": face_box}


def transposed(state_adj, band):
    cell_count = state_adj.shape[1]
    padded = jnp.pad(state_adj, ((0, 0), (2, 2)))
    band_sum = jnp.zeros(state_adj.shape, jnp.float32)
    for offset_k in range(BAND):
        shifted = padded[:, offset_k:offset_k + cell_count]
        band_sum = band_sum + jnp.sum(band[offset_k].astype(jnp.float32) * shifted[:, None, :], axis=0)
    return band_sum


def reference(adjoint, gradient, precond, band, face_jac, face_cell, face_box):
    state_adj = adjoint
    for sweep_index in range(SWEEPS):
        state_adj = state_adj + precond * (gradient - transposed(state_adj, band))
    face_ids = jnp.arange(FACES, dtype=jnp.int32)
    group_of = face_ids // (FACE_DEV * N_DOM)
    cell_ids = (group_of * (CELL_DEV * N_DOM) + face_cell).astype(jnp.int32)
    face_psi = jnp.take(state_adj, cell_ids, axis=1)
    jacobian = face_jac.astype(jnp.float32).reshape(FACES, NVAR, SENS)
    rows = jnp.sum(face_psi.T[:, :, None] * jacobian, axis=1)
    box_ids = (group_of * N_DOM + face_box[:, 0]).astype(jnp.int32)
    box_sens = jax.ops.segment_sum(rows, box_ids, num_segments=BOXES)
    return state_adj, box_sens
```

```python
import functools

import jax
import jax.numpy as jnp
from jax import lax
from jax.experimental import pallas as pl
from jax.experimental.pallas import tpu as pltpu
from jax.sharding import PartitionSpec as P

NVAR = 6
SENS = 128
BAND = 5
SWEEPS = 3
CAP = 64
LANES = 128
X, Y = 4, 8
MESH = pl.DeviceIdType.MESH

FAR_FIRST = sorted(
    range(1, X * Y),
    key=lambda s: -(min(s % X, X - s % X) + min(s // X, Y - s // X)),
)


def take_lanes(values, index):
    return jnp.take_along_axis(values, index, axis=1, mode="promise_in_bounds")


def kernel(
    groups,
    adj_h,
    grad_h,
    pre_h,
    band_h,
    jac_h,
    cell_h,
    box_h,
    adj_o,
    box_o,
    adj_v,
    grad_v,
    pre_v,
    band_v,
    jac_v,
    cell_v,
    box_v,
    bandf,
    shf,
    psi8,
    out_v,
    halo_s,
    halo_l,
    halo_r,
    req_s,
    req_r,
    resp_s,
    resp_r,
    part_s,
    part_r,
    sens_v,
    in_sem,
    halo_send,
    halo_recv,
    req_send,
    req_recv,
    resp_send,
    resp_recv,
    part_send,
    part_recv,
    out_sem,
):
    cells = adj_h.shape[1]
    faces = jac_h.shape[0]
    dom_count = X * Y
    blocks = cells // LANES
    ext = cells + LANES
    g = lax.axis_index("group")
    d = lax.axis_index("dom")
    y, x = d // X, d % X
    rows = [((y + dy) % Y) * X for dy in range(Y)]
    columns = [(x + dx) % X for dx in range(X)]
    back_rows = [((y + Y - dy) % Y) * X for dy in range(Y)]
    back_columns = [(x + X - dx) % X for dx in range(X)]
    ahead = [rows[s // X] + columns[s % X] for s in range(dom_count)]
    behind = [back_rows[s // X] + back_columns[s % X] for s in range(dom_count)]
    total = groups * dom_count
    place = g * dom_count + d
    after = (place + 1) % total
    before = (place + total - 1) % total
    after_id = (after // dom_count, after % dom_count)
    before_id = (before // dom_count, before % dom_count)

    barrier = pltpu.get_barrier_semaphore()
    for target in (before_id, after_id):
        pl.semaphore_signal(barrier, inc=1, device_id=target, device_id_type=MESH)
    for s in FAR_FIRST:
        pl.semaphore_signal(
            barrier, inc=1, device_id=(g, ahead[s]), device_id_type=MESH
        )

    loads = [
        pltpu.make_async_copy(src, dst, in_sem.at[i])
        for i, (src, dst) in enumerate(
            (
                (cell_h, cell_v),
                (band_h, band_v),
                (adj_h, adj_v),
                (grad_h, grad_v),
                (pre_h, pre_v),
                (box_h, box_v),
                (jac_h, jac_v),
            )
        )
    ]
    for load in loads:
        load.start()

    loads[0].wait()
    cell = cell_v[...]
    owner, local = cell // cells, cell % cells
    far = ((owner // X - y + Y) % Y) * X + (owner % X - x + X) % X
    slots = lax.broadcasted_iota(jnp.int32, (dom_count, faces), 0)
    reads = jnp.where(slots == far, 1.0, 0.0)
    earlier = lax.broadcasted_iota(jnp.int32, (faces, faces), 0)
    later = lax.broadcasted_iota(jnp.int32, (faces, faces), 1)
    upper = jnp.where(earlier < later, 1.0, 0.0).astype(jnp.bfloat16)
    reads_b = reads.astype(jnp.bfloat16)
    counts = jnp.dot(reads_b, upper, preferred_element_type=jnp.float32)
    rank = jnp.sum(reads * counts, axis=0, keepdims=True).astype(jnp.int32)
    lines = lax.broadcasted_iota(jnp.int32, (2 * CAP, faces), 0)
    wanted = jnp.where(
        lines < CAP, (local // LANES).astype(jnp.float32), (local % LANES).astype(jnp.float32)
    )
    wanted = jnp.where(lines % CAP == rank, wanted, 0.0).astype(jnp.bfloat16)
    requests = lax.dot_general(
        reads_b, wanted, (((1,), (1,)), ((), ())), preferred_element_type=jnp.float32
    ).astype(jnp.int32)
    for s in range(dom_count):
        req_s[s] = requests[s : s + 1]

    lane = lax.broadcasted_iota(jnp.int32, (NVAR, LANES), 1)
    head = lane < CAP
    loads[1].wait()
    half = BAND * NVAR // 2
    packed = [jnp.zeros((NVAR, LANES), jnp.float32)] * 2
    for t in range(BAND * NVAR):
        tile = band_v[t // NVAR, t % NVAR].astype(jnp.float32)
        bandf[t, :, :cells] = tile
        ends = jnp.where(head, tile[:, :LANES], tile[:, cells - LANES :])
        u = t % half
        ends = pltpu.roll(ends, 8 * u + 4, 1)
        packed[t // half] = jnp.where(lane // 8 == u, ends, packed[t // half])
    halo_s[0] = packed[0]
    halo_s[1] = packed[1]
    for load in loads[2:5]:
        load.wait()
    adj, grad, pre = adj_v[...], grad_v[...], pre_v[...]
    ends = [
        jnp.where(head, v[:, :LANES], v[:, cells - LANES :]) for v in (adj, grad, pre)
    ]
    near = (lane < 16) | (lane >= 112)
    halo_s[2] = jnp.where(
        near,
        ends[0],
        jnp.where(head, pltpu.roll(ends[1], 32, 1), pltpu.roll(ends[2], 80, 1)),
    )
    psi8[NVAR:, :] = jnp.zeros((8 - NVAR, cells), jnp.float32)

    pl.semaphore_wait(barrier, dom_count + 1)

    halo_copies = []
    for i, (target, landing) in enumerate(((after_id, halo_l), (before_id, halo_r))):
        halo_copies.append(
            pltpu.make_async_remote_copy(
                src_ref=halo_s,
                dst_ref=landing,
                send_sem=halo_send.at[i],
                recv_sem=halo_recv.at[i],
                device_id=target,
                device_id_type=MESH,
            )
        )
    for copy in halo_copies:
        copy.start()

    def send(source, landing, send_sem, recv_sem, s, target):
        pltpu.make_async_remote_copy(
            src_ref=source.at[s],
            dst_ref=landing.at[s],
            send_sem=send_sem,
            recv_sem=recv_sem,
            device_id=(g, target),
            device_id_type=MESH,
        ).start()

    def wait_all(ref, sem):
        all_slots = ref.at[pl.ds(1, dom_count - 1)]
        pltpu.make_async_copy(all_slots, all_slots, sem).wait()

    for s in FAR_FIRST:
        send(req_s, req_r, req_send, req_recv, s, ahead[s])

    rank8 = jnp.broadcast_to(rank, (8, faces))
    pick = rank8 + jnp.where(
        lax.broadcasted_iota(jnp.int32, (8, faces), 0) < 4, 0, CAP
    )
    far8 = jnp.broadcast_to(far, (8, faces))
    loads[5].wait()
    box = box_v[...]
    box_far = ((box // X - y + Y) % Y) * X + (box % X - x + X) % X
    feeds = slots == box_far

    for copy in halo_copies:
        copy.wait()
    first, last = place == 0, place == total - 1
    left = jnp.where(first, 0.0, halo_l[...])
    right = jnp.where(last, 0.0, halo_r[...])
    from_left = lane % 8 < 4
    for h in range(2):
        both = jnp.where(from_left, left[h], right[h])
        for u in range(half):
            bandf[h * half + u, :, cells:] = pltpu.roll(both, LANES - (8 * u + 4), 1)
    both_psi = jnp.where(head, right[2], left[2])
    left_grad, right_grad = pltpu.roll(left[2], 96, 1), pltpu.roll(right[2], 96, 1)
    left_pre, right_pre = pltpu.roll(left[2], 48, 1), pltpu.roll(right[2], 48, 1)
    both_grad = jnp.where(head, right_grad, left_grad)
    both_pre = jnp.where(head, right_pre, left_pre)
    psi = jnp.concatenate([adj, both_psi], axis=1)
    grad = jnp.concatenate([grad, both_grad], axis=1)
    pre = jnp.concatenate([pre, both_pre], axis=1)
    for sweep in range(SWEEPS):
        width = cells if sweep == SWEEPS - 1 else ext
        for k in range(BAND):
            shf[k] = psi if k == 2 else pltpu.roll(psi, (2 - k) % ext, 1)
        total_sum = None
        for t in range(BAND * NVAR):
            k, b = t // NVAR, t % NVAR
            column = jnp.broadcast_to(shf[k, b : b + 1, :width], (NVAR, width))
            term = bandf[t, :, :width] * column
            total_sum = term if total_sum is None else total_sum + term
        psi = psi[:, :width] + pre[:, :width] * (grad[:, :width] - total_sum)
    psi8[:NVAR, :] = psi
    out_v[...] = psi
    adj_copy = pltpu.make_async_copy(out_v, adj_o, out_sem.at[0])
    adj_copy.start()

    chunks = [psi8[:, c * LANES : (c + 1) * LANES] for c in range(blocks)]
    low8 = lax.broadcasted_iota(jnp.int32, (8, LANES), 1) < CAP

    def answer(s, wish):
        turned = pltpu.roll(wish, CAP, 1)
        low1 = low8[:1]
        chunk = jnp.broadcast_to(jnp.where(low1, wish, turned), (8, LANES))
        place_in = jnp.broadcast_to(jnp.where(low1, turned, wish), (8, LANES))
        found = take_lanes(chunks[0], place_in)
        for c in range(1, blocks):
            found = jnp.where(chunk == c, take_lanes(chunks[c], place_in), found)
        both = jnp.where(low8, found, pltpu.roll(found, 5, 0))
        return both[:4]

    resp_r[0] = answer(0, req_s[0])
    wait_all(req_r, req_recv)
    step = 4
    for start in range(0, dom_count - 1, step):
        some = FAR_FIRST[start : start + step]
        for s in some:
            resp_s[s] = answer(s, req_r[s])
        for s in some:
            send(resp_s, resp_r, resp_send, resp_recv, s, behind[s])

    loads[6].wait()
    wait_all(resp_r, resp_recv)
    found = [jnp.zeros((8, LANES), jnp.float32)] * (faces // LANES)
    for s in range(dom_count):
        values = resp_r[s]
        values = jnp.concatenate([values, values], axis=0)
        for c in range(faces // LANES):
            part = slice(c * LANES, (c + 1) * LANES)
            found[c] = jnp.where(
                far8[:, part] == s, take_lanes(values, pick[:, part]), found[c]
            )
    face_psi = jnp.concatenate(found, axis=1)
    coarse = face_psi.astype(jnp.bfloat16).astype(jnp.float32)
    fine = face_psi - coarse
    sums = jnp.zeros((2 * dom_count, SENS), jnp.float32)
    for v in range(NVAR):
        row = v if v < 3 else v + 1
        weights = jnp.concatenate(
            [
                jnp.where(feeds, coarse[row : row + 1], 0.0),
                jnp.where(feeds, fine[row : row + 1], 0.0),
            ],
            axis=0,
        ).astype(jnp.bfloat16)
        sums = sums + jnp.dot(
            weights,
            jac_v[:, v * SENS : (v + 1) * SENS],
            preferred_element_type=jnp.float32,
        )
    sums = sums[:dom_count] + sums[dom_count:]
    for s in range(1, dom_count):
        part_s[s] = sums[s : s + 1]
    part_r[0] = sums[0:1]
    for s in FAR_FIRST:
        send(part_s, part_r, part_send, part_recv, s, ahead[s])
    wait_all(part_r, part_recv)
    sens_v[...] = jnp.sum(part_r[...], axis=0)
    box_copy = pltpu.make_async_copy(sens_v, box_o, out_sem.at[1])
    box_copy.start()
    wait_all(req_s, req_send)
    wait_all(resp_s, resp_send)
    wait_all(part_s, part_send)
    adj_copy.wait()
    box_copy.wait()


def solution(mesh):
    groups = mesh.shape["group"]

    def shards(adjoint, gradient, precond, band, face_jac, face_cell, face_box):
        cells = adjoint.shape[1]
        faces = face_jac.shape[0]
        dom_count = X * Y
        ext = cells + LANES
        f32 = jnp.float32
        vmem = pltpu.VMEM
        dma = pltpu.SemaphoreType.DMA
        return pl.pallas_call(
            functools.partial(kernel, groups),
            out_shape=(
                jax.ShapeDtypeStruct((NVAR, cells), f32),
                jax.ShapeDtypeStruct((1, SENS), f32),
            ),
            in_specs=[pl.BlockSpec(memory_space=pl.ANY)] * 7,
            out_specs=[pl.BlockSpec(memory_space=pl.ANY)] * 2,
            scratch_shapes=[
                vmem((NVAR, cells), f32),
                vmem((NVAR, cells), f32),
                vmem((NVAR, cells), f32),
                vmem((BAND, NVAR, NVAR, cells), jnp.bfloat16),
                vmem((faces, NVAR * SENS), jnp.bfloat16),
                vmem((1, faces), jnp.int32),
                vmem((1, faces), jnp.int32),
                vmem((BAND * NVAR, NVAR, ext), f32),
                vmem((BAND, NVAR, ext), f32),
                vmem((8, cells), f32),
                vmem((NVAR, cells), f32),
                vmem((3, NVAR, LANES), f32),
                vmem((3, NVAR, LANES), f32),
                vmem((3, NVAR, LANES), f32),
                vmem((dom_count, 1, LANES), jnp.int32),
                vmem((dom_count, 1, LANES), jnp.int32),
                vmem((dom_count, 4, LANES), f32),
                vmem((dom_count, 4, LANES), f32),
                vmem((dom_count, 1, SENS), f32),
                vmem((dom_count, 1, SENS), f32),
                vmem((1, SENS), f32),
                dma((7,)),
                dma((2,)),
                dma((2,)),
                dma,
                dma,
                dma,
                dma,
                dma,
                dma,
                dma((2,)),
            ],
            compiler_params=pltpu.CompilerParams(
                collective_id=0, has_side_effects=True
            ),
        )(
            adjoint,
            gradient,
            precond,
            band,
            face_jac,
            face_cell.reshape(1, faces),
            face_box.reshape(1, faces),
        )

    return jax.shard_map(
        shards,
        mesh=mesh,
        in_specs=(
            P(None, ("group", "dom")),
            P(None, ("group", "dom")),
            P(None, ("group", "dom")),
            P(None, None, None, ("group", "dom")),
            P(("group", "dom"), None),
            P(("group", "dom")),
            P(("group", "dom"), None),
        ),
        out_specs=(P(None, ("group", "dom")), P(("group", "dom"), None)),
        check_vma=False,
    )
```

```python
import functools

import jax
import jax.numpy as jnp
from jax import lax
from jax.experimental import pallas as pl
from jax.experimental.pallas import tpu as pltpu
from jax.sharding import PartitionSpec as P

NVAR = 6
SENS = 128
BAND = 5
SWEEPS = 3
CAP = 64
LANES = 128
X, Y = 4, 8
MESH = pl.DeviceIdType.MESH

FAR_FIRST = sorted(
    range(1, X * Y),
    key=lambda s: -(min(s % X, X - s % X) + min(s // X, Y - s // X)),
)


def take_lanes(values, index):
    return jnp.take_along_axis(values, index, axis=1, mode="promise_in_bounds")


def kernel(
    groups,
    adj_h,
    grad_h,
    pre_h,
    band_h,
    jac_h,
    cell_h,
    box_h,
    adj_o,
    box_o,
    adj_v,
    grad_v,
    pre_v,
    band_v,
    jac_v,
    cell_v,
    box_v,
    bandf,
    shf,
    psi8,
    halo_s,
    halo_l,
    halo_r,
    req_s,
    req_r,
    resp_s,
    resp_r,
    part_s,
    part_r,
    in_sem,
    halo_send,
    halo_recv,
    req_send,
    req_recv,
    resp_send,
    resp_recv,
    part_send,
    part_recv,
):
    cells = adj_h.shape[1]
    faces = jac_h.shape[0]
    dom_count = X * Y
    blocks = cells // LANES
    ext = cells + LANES
    g = lax.axis_index("group")
    d = lax.axis_index("dom")
    y, x = d // X, d % X
    rows = [((y + dy) % Y) * X for dy in range(Y)]
    columns = [(x + dx) % X for dx in range(X)]
    back_rows = [((y + Y - dy) % Y) * X for dy in range(Y)]
    back_columns = [(x + X - dx) % X for dx in range(X)]
    ahead = [rows[s // X] + columns[s % X] for s in range(dom_count)]
    behind = [back_rows[s // X] + back_columns[s % X] for s in range(dom_count)]
    total = groups * dom_count
    place = g * dom_count + d
    after = (place + 1) % total
    before = (place + total - 1) % total
    after_id = (after // dom_count, after % dom_count)
    before_id = (before // dom_count, before % dom_count)

    loads = [
        pltpu.make_async_copy(src, dst, in_sem.at[i])
        for i, (src, dst) in enumerate(
            (
                (cell_h, cell_v),
                (band_h, band_v),
                (adj_h, adj_v),
                (grad_h, grad_v),
                (pre_h, pre_v),
                (box_h, box_v),
                (jac_h, jac_v),
            )
        )
    ]
    for load in loads:
        load.start()

    barrier = pltpu.get_barrier_semaphore()
    first, last = place == 0, place == total - 1

    @pl.when(jnp.logical_not(first))
    def _():
        pl.semaphore_signal(barrier, inc=1, device_id=before_id, device_id_type=MESH)

    @pl.when(jnp.logical_not(last))
    def _():
        pl.semaphore_signal(barrier, inc=1, device_id=after_id, device_id_type=MESH)

    for s in FAR_FIRST:
        pl.semaphore_signal(
            barrier, inc=1, device_id=(g, ahead[s]), device_id_type=MESH
        )

    loads[0].wait()
    cell = cell_v[...]
    owner, local = cell // cells, cell % cells
    far = ((owner // X - y + Y) % Y) * X + (owner % X - x + X) % X
    slots = lax.broadcasted_iota(jnp.int32, (dom_count, faces), 0)
    reads = jnp.where(slots == far, 1.0, 0.0)
    earlier = lax.broadcasted_iota(jnp.int32, (faces, faces), 0)
    later = lax.broadcasted_iota(jnp.int32, (faces, faces), 1)
    upper = jnp.where(earlier < later, 1.0, 0.0).astype(jnp.bfloat16)
    reads_b = reads.astype(jnp.bfloat16)
    counts = jnp.dot(reads_b, upper, preferred_element_type=jnp.float32)
    rank = jnp.sum(reads * counts, axis=0, keepdims=True).astype(jnp.int32)
    lines = lax.broadcasted_iota(jnp.int32, (2 * CAP, faces), 0)
    wanted = jnp.where(
        lines < CAP, (local // LANES).astype(jnp.float32), (local % LANES).astype(jnp.float32)
    )
    wanted = jnp.where(lines % CAP == rank, wanted, 0.0).astype(jnp.bfloat16)
    requests = lax.dot_general(
        reads_b, wanted, (((1,), (1,)), ((), ())), preferred_element_type=jnp.float32
    ).astype(jnp.int32)
    for s in range(dom_count):
        req_s[s] = requests[s : s + 1]

    lane = lax.broadcasted_iota(jnp.int32, (NVAR, LANES), 1)
    head = lane < CAP
    loads[1].wait()
    half = BAND * NVAR // 2
    packed = [jnp.zeros((NVAR, LANES), jnp.float32)] * 2
    for t in range(BAND * NVAR):
        tile = band_v[t // NVAR, t % NVAR].astype(jnp.float32)
        bandf[t, :, :cells] = tile
        ends = jnp.where(head, tile[:, :LANES], tile[:, cells - LANES :])
        u = t % half
        ends = pltpu.roll(ends, 8 * u + 4, 1)
        packed[t // half] = jnp.where(lane // 8 == u, ends, packed[t // half])
    rest = jnp.zeros((8 - NVAR, LANES), jnp.float32)
    halo_s[0] = jnp.concatenate([packed[0], rest], axis=0)
    halo_s[1] = jnp.concatenate([packed[1], rest], axis=0)
    for load in loads[2:5]:
        load.wait()
    adj, grad, pre = adj_v[...], grad_v[...], pre_v[...]
    ends = [
        jnp.where(head, v[:, :LANES], v[:, cells - LANES :]) for v in (adj, grad, pre)
    ]
    near = (lane < 16) | (lane >= 112)
    packed = jnp.where(
        near,
        ends[0],
        jnp.where(head, pltpu.roll(ends[1], 32, 1), pltpu.roll(ends[2], 80, 1)),
    )
    halo_s[2] = jnp.concatenate([packed, rest], axis=0)
    psi8[NVAR:, :] = jnp.zeros((8 - NVAR, cells), jnp.float32)

    ends_of_all = first.astype(jnp.int32) + last.astype(jnp.int32)
    pl.semaphore_wait(barrier, dom_count + 1 - ends_of_all)

    @pl.when(first)
    def _():
        halo_l[...] = jnp.zeros_like(halo_l)

    @pl.when(last)
    def _():
        halo_r[...] = jnp.zeros_like(halo_r)

    halo_copies = []
    for i, (target, landing) in enumerate(((after_id, halo_l), (before_id, halo_r))):
        halo_copies.append(
            pltpu.make_async_remote_copy(
                src_ref=halo_s,
                dst_ref=landing,
                send_sem=halo_send.at[i],
                recv_sem=halo_recv.at[i],
                device_id=target,
                device_id_type=MESH,
            )
        )
    pl.when(jnp.logical_not(last))(halo_copies[0].start)
    pl.when(jnp.logical_not(first))(halo_copies[1].start)

    def send(source, landing, send_sem, recv_sem, s, target):
        pltpu.make_async_remote_copy(
            src_ref=source.at[s],
            dst_ref=landing.at[s],
            send_sem=send_sem,
            recv_sem=recv_sem,
            device_id=(g, target),
            device_id_type=MESH,
        ).start()

    def wait_all(ref, sem):
        all_slots = ref.at[pl.ds(1, dom_count - 1)]
        pltpu.make_async_copy(all_slots, all_slots, sem).wait()

    for s in FAR_FIRST:
        send(req_s, req_r, req_send, req_recv, s, ahead[s])

    rank8 = jnp.broadcast_to(rank, (8, faces))
    pick = rank8 + jnp.where(
        lax.broadcasted_iota(jnp.int32, (8, faces), 0) < 4, 0, CAP
    )
    far8 = jnp.broadcast_to(far, (8, faces))
    loads[5].wait()
    box = box_v[...]
    box_far = ((box // X - y + Y) % Y) * X + (box % X - x + X) % X
    feeds = slots == box_far

    pl.when(jnp.logical_not(first))(halo_copies[0].wait_recv)
    pl.when(jnp.logical_not(last))(halo_copies[1].wait_recv)
    left = halo_l[:, :NVAR, :]
    right = halo_r[:, :NVAR, :]
    from_left = lane % 8 < 4
    for h in range(2):
        both = jnp.where(from_left, left[h], right[h])
        for u in range(half):
            bandf[h * half + u, :, cells:] = pltpu.roll(both, LANES - (8 * u + 4), 1)
    both_psi = jnp.where(head, right[2], left[2])
    left_grad, right_grad = pltpu.roll(left[2], 96, 1), pltpu.roll(right[2], 96, 1)
    left_pre, right_pre = pltpu.roll(left[2], 48, 1), pltpu.roll(right[2], 48, 1)
    both_grad = jnp.where(head, right_grad, left_grad)
    both_pre = jnp.where(head, right_pre, left_pre)
    psi = jnp.concatenate([adj, both_psi], axis=1)
    grad = jnp.concatenate([grad, both_grad], axis=1)
    pre = jnp.concatenate([pre, both_pre], axis=1)
    for sweep in range(SWEEPS):
        width = cells if sweep == SWEEPS - 1 else ext
        for k in range(BAND):
            shf[k] = psi if k == 2 else pltpu.roll(psi, (2 - k) % ext, 1)
        total_sum = None
        for t in range(BAND * NVAR):
            k, b = t // NVAR, t % NVAR
            column = jnp.broadcast_to(shf[k, b : b + 1, :width], (NVAR, width))
            term = bandf[t, :, :width] * column
            total_sum = term if total_sum is None else total_sum + term
        psi = psi[:, :width] + pre[:, :width] * (grad[:, :width] - total_sum)
    psi8[:NVAR, :] = psi
    adj_o[...] = psi

    chunks = [psi8[:, c * LANES : (c + 1) * LANES] for c in range(blocks)]
    low8 = lax.broadcasted_iota(jnp.int32, (8, LANES), 1) < CAP

    low1 = low8[:1]

    def answers(wish, other):
        chunk = jnp.where(low1, wish, pltpu.roll(other, CAP, 1))
        place_in = jnp.where(low1, pltpu.roll(wish, CAP, 1), other)
        chunk = jnp.broadcast_to(chunk, (8, LANES))
        place_in = jnp.broadcast_to(place_in, (8, LANES))
        found = take_lanes(chunks[0], place_in)
        for c in range(1, blocks):
            found = jnp.where(chunk == c, take_lanes(chunks[c], place_in), found)
        turned = pltpu.roll(found, 5, 0)
        return (
            jnp.where(low8, found, pltpu.roll(turned, CAP, 1))[:4],
            jnp.where(low8, pltpu.roll(found, CAP, 1), turned)[:4],
        )

    wait_all(req_r, req_recv)
    order = FAR_FIRST + [0]
    step = 8
    for start in range(0, dom_count, step):
        some = order[start : start + step]
        for s, t in zip(some[::2], some[1::2]):
            resp_s[s], own = answers(req_r[s], req_r[t] if t else req_s[0])
            if t:
                resp_s[t] = own
            else:
                resp_r[0] = own
        for s in some:
            if s:
                send(resp_s, resp_r, resp_send, resp_recv, s, behind[s])

    loads[6].wait()
    wait_all(resp_r, resp_recv)
    found = [jnp.zeros((8, LANES), jnp.float32)] * (faces // LANES)
    for s in range(dom_count):
        values = resp_r[s]
        values = jnp.concatenate([values, values], axis=0)
        for c in range(faces // LANES):
            part = slice(c * LANES, (c + 1) * LANES)
            found[c] = jnp.where(
                far8[:, part] == s, take_lanes(values, pick[:, part]), found[c]
            )
    face_psi = jnp.concatenate(found, axis=1)
    coarse = face_psi.astype(jnp.bfloat16).astype(jnp.float32)
    fine = face_psi - coarse
    sums = jnp.zeros((2 * dom_count, SENS), jnp.float32)
    for v in range(NVAR):
        row = v if v < 3 else v + 1
        weights = jnp.concatenate(
            [
                jnp.where(feeds, coarse[row : row + 1], 0.0),
                jnp.where(feeds, fine[row : row + 1], 0.0),
            ],
            axis=0,
        ).astype(jnp.bfloat16)
        sums = sums + jnp.dot(
            weights,
            jac_v[:, v * SENS : (v + 1) * SENS],
            preferred_element_type=jnp.float32,
        )
    sums = sums[:dom_count] + sums[dom_count:]
    for s in range(1, dom_count):
        part_s[s] = sums[s : s + 1]
    part_r[0] = sums[0:1]
    for s in FAR_FIRST:
        send(part_s, part_r, part_send, part_recv, s, ahead[s])
    wait_all(part_r, part_recv)
    box_o[...] = jnp.sum(part_r[...], axis=0)
    wait_all(req_s, req_send)
    wait_all(resp_s, resp_send)
    wait_all(part_s, part_send)
    pl.when(jnp.logical_not(last))(halo_copies[0].wait_send)
    pl.when(jnp.logical_not(first))(halo_copies[1].wait_send)


def solution(mesh):
    groups = mesh.shape["group"]

    def shards(adjoint, gradient, precond, band, face_jac, face_cell, face_box):
        cells = adjoint.shape[1]
        faces = face_jac.shape[0]
        dom_count = X * Y
        ext = cells + LANES
        f32 = jnp.float32
        vmem = pltpu.VMEM
        dma = pltpu.SemaphoreType.DMA
        return pl.pallas_call(
            functools.partial(kernel, groups),
            out_shape=(
                vmem((NVAR, cells), f32),
                vmem((1, SENS), f32),
            ),
            in_specs=[pl.BlockSpec(memory_space=pl.ANY)] * 7,
            out_specs=[pl.BlockSpec(memory_space=pltpu.VMEM)] * 2,
            scratch_shapes=[
                vmem((NVAR, cells), f32),
                vmem((NVAR, cells), f32),
                vmem((NVAR, cells), f32),
                vmem((BAND, NVAR, NVAR, cells), jnp.bfloat16),
                vmem((faces, NVAR * SENS), jnp.bfloat16),
                vmem((1, faces), jnp.int32),
                vmem((1, faces), jnp.int32),
                vmem((BAND * NVAR, NVAR, ext), f32),
                vmem((BAND, NVAR, ext), f32),
                vmem((8, cells), f32),
                vmem((3, 8, LANES), f32),
                vmem((3, 8, LANES), f32),
                vmem((3, 8, LANES), f32),
                vmem((dom_count, 1, LANES), jnp.int32),
                vmem((dom_count, 1, LANES), jnp.int32),
                vmem((dom_count, 4, LANES), f32),
                vmem((dom_count, 4, LANES), f32),
                vmem((dom_count, 1, SENS), f32),
                vmem((dom_count, 1, SENS), f32),
                dma((7,)),
                dma((2,)),
                dma((2,)),
                dma,
                dma,
                dma,
                dma,
                dma,
                dma,
            ],
            compiler_params=pltpu.CompilerParams(
                collective_id=0, has_side_effects=True
            ),
        )(
            adjoint,
            gradient,
            precond,
            band,
            face_jac,
            face_cell.reshape(1, faces),
            face_box.reshape(1, faces),
        )

    return jax.shard_map(
        shards,
        mesh=mesh,
        in_specs=(
            P(None, ("group", "dom")),
            P(None, ("group", "dom")),
            P(None, ("group", "dom")),
            P(None, None, None, ("group", "dom")),
            P(("group", "dom"), None),
            P(("group", "dom")),
            P(("group", "dom"), None),
        ),
        out_specs=(P(None, ("group", "dom")), P(("group", "dom"), None)),
        check_vma=False,
    )
```

```python
import functools

import jax
import jax.numpy as jnp
from jax import lax
from jax.experimental import pallas as pl
from jax.experimental.pallas import tpu as pltpu
from jax.sharding import PartitionSpec as P

NVAR = 6
SENS = 128
BAND = 5
SWEEPS = 3
CAP = 64
LANES = 128
X, Y = 4, 8
MESH = pl.DeviceIdType.MESH

FAR_FIRST = sorted(
    range(1, X * Y),
    key=lambda s: -(min(s % X, X - s % X) + min(s // X, Y - s // X)),
)
NEAR, FAR = (6, 7, 1, 2), (3, 4, 5)
SLOT = {dy: i for i, dy in enumerate(NEAR + FAR)}


def take_lanes(values, index):
    return jnp.take_along_axis(values, index, axis=1, mode="promise_in_bounds")


def sweep(psi, grad, pre, band_ref, shifted_ref, width):
    for _ in range(SWEEPS):
        for k in range(BAND):
            shifted_ref[k, :, :width] = (
                psi if k == 2 else pltpu.roll(psi, (2 - k) % width, 1)
            )
        sums = []
        for k in range(BAND):
            part = None
            for b in range(NVAR):
                column = jnp.broadcast_to(
                    shifted_ref[k, b : b + 1, :width], (NVAR, width)
                )
                term = band_ref[k * NVAR + b] * column
                part = term if part is None else part + term
            sums.append(part)
        total = (sums[0] + sums[1]) + (sums[2] + sums[3]) + sums[4]
        psi = psi + pre * (grad - total)
    return psi


def kernel(
    groups,
    adj_h,
    grad_h,
    pre_h,
    band_h,
    jac_h,
    cell_h,
    box_h,
    out_o,
    adj_v,
    grad_v,
    pre_v,
    band_v,
    jac_v,
    cell_v,
    box_v,
    bandf,
    band_edge,
    shf,
    halo_s,
    halo_l,
    halo_r,
    psi_s,
    psi_r,
    req_s,
    req_r,
    req_own,
    resp_s,
    resp_r,
    resp_own,
    part_s,
    part_r,
    in_sem,
    halo_send,
    halo_recv,
    known,
    psi_send,
    psi_recv,
    req_send,
    req_recv,
    resp_send,
    resp_recv,
    part_send,
    part_recv,
):
    cells = adj_h.shape[1]
    faces = jac_h.shape[0]
    dom_count = X * Y
    blocks = cells // LANES
    tiles = blocks * NVAR // 8
    g = lax.axis_index("group")
    d = lax.axis_index("dom")
    y, x = d // X, d % X
    rows = [((y + dy) % Y) * X for dy in range(Y)]
    columns = [(x + dx) % X for dx in range(X)]
    ahead = [rows[s // X] + columns[s % X] for s in range(dom_count)]
    total = groups * dom_count
    place = g * dom_count + d
    after = (place + 1) % total
    before = (place + total - 1) % total
    after_id = (after // dom_count, after % dom_count)
    before_id = (before // dom_count, before % dom_count)
    first, last = place == 0, place == total - 1

    loads = [
        pltpu.make_async_copy(src, dst, in_sem.at[i])
        for i, (src, dst) in enumerate(
            (
                (band_h, band_v),
                (adj_h, adj_v),
                (grad_h, grad_v),
                (pre_h, pre_v),
                (cell_h, cell_v),
                (box_h, box_v),
                (jac_h, jac_v),
            )
        )
    ]
    for load in loads:
        load.start()

    barrier = pltpu.get_barrier_semaphore()

    def greet(target):
        pl.semaphore_signal(barrier, inc=1, device_id=target, device_id_type=MESH)

    near = [X * dy for dy in NEAR] + list(range(1, X))
    for s in near:
        greet((g, ahead[s]))
    pl.when(jnp.logical_not(first))(lambda: greet(before_id))
    pl.when(jnp.logical_not(last))(lambda: greet(after_id))

    lane = lax.broadcasted_iota(jnp.int32, (NVAR, LANES), 1)
    head = lane < CAP
    half = BAND * NVAR // 2
    packed = [jnp.zeros((NVAR, LANES), jnp.float32)] * 2
    loads[0].wait()
    for t in range(BAND * NVAR):
        tile = band_v[t // NVAR, t % NVAR].astype(jnp.float32)
        bandf[t] = tile
        start, end = tile[:, :LANES], tile[:, cells - LANES :]
        band_edge[t, :, :LANES] = end
        band_edge[t, :, 2 * LANES :] = start
        u = t % half
        ends = pltpu.roll(jnp.where(head, start, end), 8 * u + 4, 1)
        packed[t // half] = jnp.where(lane // 8 == u, ends, packed[t // half])
    rest = jnp.zeros((8 - NVAR, LANES), jnp.float32)
    halo_s[0] = jnp.concatenate([packed[0], rest], axis=0)
    halo_s[1] = jnp.concatenate([packed[1], rest], axis=0)
    for load in loads[1:4]:
        load.wait()
    adj, grad, pre = adj_v[...], grad_v[...], pre_v[...]
    ends = [
        jnp.where(head, v[:, :LANES], v[:, cells - LANES :]) for v in (adj, grad, pre)
    ]
    packed = jnp.where(
        (lane < 16) | (lane >= 112),
        ends[0],
        jnp.where(head, pltpu.roll(ends[1], 32, 1), pltpu.roll(ends[2], 80, 1)),
    )
    halo_s[2] = jnp.concatenate([packed, rest], axis=0)

    @pl.when(first)
    def _():
        halo_l[...] = jnp.zeros_like(halo_l)

    @pl.when(last)
    def _():
        halo_r[...] = jnp.zeros_like(halo_r)

    missing = first.astype(jnp.int32) + last.astype(jnp.int32)
    pl.semaphore_wait(barrier, len(near) + 2 - missing)

    halo_copies = []
    for i, (target, landing) in enumerate(((after_id, halo_l), (before_id, halo_r))):
        halo_copies.append(
            pltpu.make_async_remote_copy(
                src_ref=halo_s,
                dst_ref=landing,
                send_sem=halo_send.at[i],
                recv_sem=halo_recv.at[i],
                device_id=target,
                device_id_type=MESH,
            )
        )
    pl.when(jnp.logical_not(last))(halo_copies[0].start)
    pl.when(jnp.logical_not(first))(halo_copies[1].start)

    for dy in (2, 6):
        pl.semaphore_signal(
            known, inc=1, device_id=(g, ahead[X * dy]), device_id_type=MESH
        )

    loads[4].wait()
    cell = cell_v[...]
    owner, local = cell // cells, cell % cells
    far = ((owner // X - y + Y) % Y) * X + (owner % X - x + X) % X
    slots = lax.broadcasted_iota(jnp.int32, (dom_count, faces), 0)
    reads = jnp.where(slots == far, 1.0, 0.0)
    earlier = lax.broadcasted_iota(jnp.int32, (faces, faces), 0)
    later = lax.broadcasted_iota(jnp.int32, (faces, faces), 1)
    upper = jnp.where(earlier < later, 1.0, 0.0).astype(jnp.bfloat16)
    reads_b = reads.astype(jnp.bfloat16)
    counts = jnp.dot(reads_b, upper, preferred_element_type=jnp.float32)
    rank = jnp.sum(reads * counts, axis=0, keepdims=True).astype(jnp.int32)
    lines = lax.broadcasted_iota(jnp.int32, (2 * CAP, faces), 0)
    wanted = jnp.where(
        lines < CAP, (local // LANES).astype(jnp.float32), (local % LANES).astype(jnp.float32)
    )
    wanted = jnp.where(lines % CAP == rank, wanted, 0.0).astype(jnp.bfloat16)
    requests = lax.dot_general(
        reads_b, wanted, (((1,), (1,)), ((), ())), preferred_element_type=jnp.float32
    ).astype(jnp.int32)
    req_own[...] = requests[:X]
    for dy in range(1, Y):
        req_s[SLOT[dy]] = requests[X * dy : X * dy + X]

    def send(source, landing, send_sem, recv_sem, target):
        pltpu.make_async_remote_copy(
            src_ref=source,
            dst_ref=landing,
            send_sem=send_sem,
            recv_sem=recv_sem,
            device_id=(g, target),
            device_id_type=MESH,
        ).start()

    def wait_all(ref, start, count, sem):
        some = ref.at[pl.ds(start, count)]
        pltpu.make_async_copy(some, some, sem).wait()

    pl.semaphore_wait(known, 2)
    for dy in (4, 3, 5, 2, 6, 1, 7):
        i = SLOT[dy]
        send(req_s.at[i], req_r.at[i], req_send, req_recv, ahead[X * dy])

    inner = sweep(adj, grad, pre, bandf, shf, cells)

    pick = jnp.broadcast_to(rank, (8, faces)) + jnp.where(
        lax.broadcasted_iota(jnp.int32, (8, faces), 0) < 3, 0, CAP
    )
    far8 = jnp.broadcast_to(far, (8, faces))
    loads[5].wait()
    box = box_v[...]
    box_far = ((box // X - y + Y) % Y) * X + (box % X - x + X) % X
    feeds = slots == box_far

    pl.when(jnp.logical_not(first))(halo_copies[0].wait_recv)
    pl.when(jnp.logical_not(last))(halo_copies[1].wait_recv)
    left = halo_l[:, :NVAR, :]
    right = halo_r[:, :NVAR, :]
    from_left = lane % 8 < 4
    for h in range(2):
        both = jnp.where(from_left, left[h], right[h])
        for u in range(half):
            band_edge[h * half + u, :, LANES : 2 * LANES] = pltpu.roll(
                both, LANES - (8 * u + 4), 1
            )

    def edge(v, turn):
        between = jnp.where(head, right[2], left[2])
        if turn:
            between = jnp.where(
                head, pltpu.roll(right[2], turn, 1), pltpu.roll(left[2], turn, 1)
            )
        return jnp.concatenate(
            [v[:, cells - LANES :], between, v[:, :LANES]], axis=1
        )

    outer = sweep(
        edge(adj, 0), edge(grad, 96), edge(pre, 48), band_edge, shf, 3 * LANES
    )
    psi = [inner[:, c * LANES : (c + 1) * LANES] for c in range(blocks)]
    psi[0] = jnp.where(head, outer[:, 2 * LANES :], psi[0])
    psi[-1] = jnp.where(head, psi[-1], outer[:, :LANES])
    spare = jnp.concatenate(psi[tiles:], axis=0)
    for c in range(tiles):
        part = slice(c * LANES, (c + 1) * LANES)
        psi_s[:, part] = jnp.concatenate([psi[c], spare[2 * c : 2 * c + 2]], axis=0)
    for dx in (2, 1, 3):
        i = X - dx
        send(psi_s, psi_r.at[i], psi_send, psi_recv, ahead[dx])
    for c in range(blocks):
        out_o[:NVAR, c * LANES : (c + 1) * LANES] = psi[c]
    out_o[NVAR:, :] = jnp.zeros((8 - NVAR, cells), jnp.float32)

    low8 = lax.broadcasted_iota(jnp.int32, (8, LANES), 1) < CAP
    low1 = low8[:1]

    def row_values(ref):
        parts = [ref[:, c * LANES : (c + 1) * LANES] for c in range(tiles)]
        size = 8 - NVAR
        for start in range(0, tiles, NVAR // size):
            some = [p[NVAR:] for p in parts[start : start + NVAR // size]]
            parts.append(jnp.concatenate(some + some[:1], axis=0))
        return parts

    def answers(values, wish, other):
        chunk = jnp.where(low1, wish, pltpu.roll(other, CAP, 1))
        place_in = jnp.where(low1, pltpu.roll(wish, CAP, 1), other)
        chunk = jnp.broadcast_to(chunk, (8, LANES))
        place_in = jnp.broadcast_to(place_in, (8, LANES))
        found = take_lanes(values[0], place_in)
        for c in range(1, blocks):
            found = jnp.where(chunk == c, take_lanes(values[c], place_in), found)
        turned = pltpu.roll(found, 5, 0)
        return (
            jnp.where(low8, found, pltpu.roll(turned, CAP, 1))[:3],
            jnp.where(low8, pltpu.roll(found, CAP, 1), turned)[:3],
        )

    pairs = ((4, 3), (5, 2), (6, 1), (7, 0))

    def answer(values, dx, pair):
        a, b = pair
        wish = req_r[SLOT[a], dx : dx + 1]
        other = req_r[SLOT[b], dx : dx + 1] if b else req_own[dx : dx + 1]
        one, two = answers(values, wish, other)
        resp_s[SLOT[a], 3 * dx : 3 * dx + 3] = one
        if b:
            resp_s[SLOT[b], 3 * dx : 3 * dx + 3] = two
        else:
            resp_own[3 * dx : 3 * dx + 3] = two

    wait_all(req_r, 0, Y - 1, req_recv)
    own_values = row_values(psi_s)
    for pair in pairs:
        answer(own_values, 0, pair)
    wait_all(psi_r, 1, X - 1, psi_recv)
    values = [row_values(psi_r.at[dx]) for dx in range(1, X)]
    for pair in pairs:
        for dx in range(1, X):
            answer(values[dx - 1], dx, pair)
        for dy in pair:
            if dy:
                i = SLOT[dy]
                send(
                    resp_s.at[i],
                    resp_r.at[i],
                    resp_send,
                    resp_recv.at[0 if dy in NEAR else 1],
                    ahead[X * (Y - dy)],
                )

    found = [jnp.zeros((8, LANES), jnp.float32)] * (faces // LANES)

    def look(dy, ref):
        for dx in range(X):
            got = ref[3 * dx : 3 * dx + 3]
            got = jnp.concatenate([got, got, got[:2]], axis=0)
            for c in range(faces // LANES):
                part = slice(c * LANES, (c + 1) * LANES)
                found[c] = jnp.where(
                    far8[:, part] == dy * X + dx, take_lanes(got, pick[:, part]), found[c]
                )

    look(0, resp_own)
    wait_all(resp_r, 0, len(NEAR), resp_recv.at[0])
    for dy in NEAR:
        look(dy, resp_r.at[SLOT[dy]])
    loads[6].wait()
    wait_all(resp_r, len(NEAR), len(FAR), resp_recv.at[1])
    for dy in FAR:
        look(dy, resp_r.at[SLOT[dy]])
    face_psi = jnp.concatenate(found, axis=1)
    coarse = face_psi.astype(jnp.bfloat16).astype(jnp.float32)
    fine = face_psi - coarse
    sums = jnp.zeros((2 * dom_count, SENS), jnp.float32)
    for v in range(NVAR):
        weights = jnp.concatenate(
            [
                jnp.where(feeds, coarse[v : v + 1], 0.0),
                jnp.where(feeds, fine[v : v + 1], 0.0),
            ],
            axis=0,
        ).astype(jnp.bfloat16)
        sums = sums + jnp.dot(
            weights,
            jac_v[:, v * SENS : (v + 1) * SENS],
            preferred_element_type=jnp.float32,
        )
    sums = sums[:dom_count] + sums[dom_count:]
    for s in range(1, dom_count):
        part_s[s] = sums[s : s + 1]
    part_r[0] = sums[0:1]
    for s in FAR_FIRST:
        send(part_s.at[s], part_r.at[s], part_send, part_recv, ahead[s])
    wait_all(part_r, 1, dom_count - 1, part_recv)
    out_o[NVAR : NVAR + 1, :SENS] = jnp.sum(part_r[...], axis=0)
    pl.when(jnp.logical_not(last))(halo_copies[0].wait_send)
    pl.when(jnp.logical_not(first))(halo_copies[1].wait_send)
    wait_all(req_s, 0, Y - 1, req_send)
    wait_all(psi_r, 1, X - 1, psi_send)
    wait_all(resp_s, 0, Y - 1, resp_send)
    wait_all(part_s, 1, dom_count - 1, part_send)


def solution(mesh):
    groups = mesh.shape["group"]

    def shards(adjoint, gradient, precond, band, face_jac, face_cell, face_box):
        cells = adjoint.shape[1]
        faces = face_jac.shape[0]
        dom_count = X * Y
        packed = cells * NVAR // 8
        f32 = jnp.float32
        vmem = pltpu.VMEM
        dma = pltpu.SemaphoreType.DMA
        out = pl.pallas_call(
            functools.partial(kernel, groups),
            out_shape=vmem((8, cells), f32),
            in_specs=[pl.BlockSpec(memory_space=pl.ANY)] * 7,
            out_specs=pl.BlockSpec(memory_space=pltpu.VMEM),
            scratch_shapes=[
                vmem((NVAR, cells), f32),
                vmem((NVAR, cells), f32),
                vmem((NVAR, cells), f32),
                vmem((BAND, NVAR, NVAR, cells), jnp.bfloat16),
                vmem((faces, NVAR * SENS), jnp.bfloat16),
                vmem((1, faces), jnp.int32),
                vmem((1, faces), jnp.int32),
                vmem((BAND * NVAR, NVAR, cells), f32),
                vmem((BAND * NVAR, NVAR, 3 * LANES), f32),
                vmem((BAND, NVAR, cells), f32),
                vmem((3, 8, LANES), f32),
                vmem((3, 8, LANES), f32),
                vmem((3, 8, LANES), f32),
                vmem((8, packed), f32),
                vmem((X, 8, packed), f32),
                vmem((Y - 1, X, LANES), jnp.int32),
                vmem((Y - 1, X, LANES), jnp.int32),
                vmem((X, LANES), jnp.int32),
                vmem((Y - 1, 3 * X, LANES), f32),
                vmem((Y - 1, 3 * X, LANES), f32),
                vmem((3 * X, LANES), f32),
                vmem((dom_count, 1, LANES), f32),
                vmem((dom_count, 1, LANES), f32),
                dma((7,)),
                dma((2,)),
                dma((2,)),
                pltpu.SemaphoreType.REGULAR,
                dma,
                dma,
                dma,
                dma,
                dma,
                dma((2,)),
                dma,
                dma,
            ],
            compiler_params=pltpu.CompilerParams(
                collective_id=0, has_side_effects=True
            ),
        )(
            adjoint,
            gradient,
            precond,
            band,
            face_jac,
            face_cell.reshape(1, faces),
            face_box.reshape(1, faces),
        )
        return out[:NVAR], out[NVAR : NVAR + 1, :SENS]

    return jax.shard_map(
        shards,
        mesh=mesh,
        in_specs=(
            P(None, ("group", "dom")),
            P(None, ("group", "dom")),
            P(None, ("group", "dom")),
            P(None, None, None, ("group", "dom")),
            P(("group", "dom"), None),
            P(("group", "dom")),
            P(("group", "dom"), None),
        ),
        out_specs=(P(None, ("group", "dom")), P(("group", "dom"), None)),
        check_vma=False,
    )
```

```python
import functools

import jax
import jax.numpy as jnp
from jax import lax
from jax.experimental import pallas as pl
from jax.experimental.pallas import tpu as pltpu
from jax.sharding import PartitionSpec as P

NVAR = 6
SENS = 128
BAND = 5
SWEEPS = 3
CAP = 64
HALO = 2 * SWEEPS
LANES = 128
X, Y = 4, 8
MESH = pl.DeviceIdType.MESH

FAR_FIRST = sorted(
    range(1, X * Y),
    key=lambda s: -(min(s % X, X - s % X) + min(s // X, Y - s // X)),
)
NEAR, FAR = (6, 7, 1, 2), (3, 4, 5)
SLOT = {dy: i for i, dy in enumerate(NEAR + FAR)}


def take_lanes(values, index):
    return jnp.take_along_axis(values, index, axis=1, mode="promise_in_bounds")


def sweep(psi, grad, pre, band_ref, shifted_ref, width):
    for _ in range(SWEEPS):
        for k in range(BAND):
            shifted_ref[k, :, :width] = (
                psi if k == 2 else pltpu.roll(psi, (2 - k) % width, 1)
            )
        sums = []
        for k in range(BAND):
            part = None
            for b in range(NVAR):
                column = jnp.broadcast_to(
                    shifted_ref[k, b : b + 1, :width], (NVAR, width)
                )
                term = band_ref[k * NVAR + b] * column
                part = term if part is None else part + term
            sums.append(part)
        total = (sums[0] + sums[1]) + (sums[2] + sums[3]) + sums[4]
        psi = psi + pre * (grad - total)
    return psi


def kernel(
    groups,
    adj_h,
    grad_h,
    pre_h,
    band_h,
    jac_h,
    cell_h,
    box_h,
    out_o,
    adj_v,
    grad_v,
    pre_v,
    band_v,
    jac_v,
    cell_v,
    box_v,
    bandf,
    band_edge,
    shf,
    halo_s,
    halo_l,
    halo_r,
    psi_s,
    psi_r,
    req_s,
    req_r,
    req_own,
    resp_s,
    resp_r,
    resp_own,
    ends_s,
    ends_r,
    part_s,
    part_r,
    in_sem,
    halo_send,
    halo_recv,
    psi_send,
    psi_recv,
    req_send,
    req_recv,
    resp_send,
    resp_recv,
    ends_send,
    ends_recv,
    part_send,
    part_recv,
):
    cells = adj_h.shape[1]
    faces = jac_h.shape[0]
    dom_count = X * Y
    blocks = cells // LANES
    tiles = blocks * NVAR // 8
    g = lax.axis_index("group")
    d = lax.axis_index("dom")
    y, x = d // X, d % X
    rows = [((y + dy) % Y) * X for dy in range(Y)]
    columns = [(x + dx) % X for dx in range(X)]
    ahead = [rows[s // X] + columns[s % X] for s in range(dom_count)]
    total = groups * dom_count
    place = g * dom_count + d
    after = (place + 1) % total
    before = (place + total - 1) % total
    after_id = (after // dom_count, after % dom_count)
    before_id = (before // dom_count, before % dom_count)
    first, last = place == 0, place == total - 1

    loads = [
        pltpu.make_async_copy(src, dst, in_sem.at[i])
        for i, (src, dst) in enumerate(
            (
                (band_h, band_v),
                (adj_h, adj_v),
                (grad_h, grad_v),
                (pre_h, pre_v),
                (cell_h, cell_v),
                (box_h, box_v),
                (jac_h, jac_v),
            )
        )
    ]
    for load in loads:
        load.start()

    barrier = pltpu.get_barrier_semaphore()

    def greet(target):
        pl.semaphore_signal(barrier, inc=1, device_id=target, device_id_type=MESH)

    lines = [X * dy for dy in (4, 3, 5, 2, 6, 1, 7)] + [2, 1, 3]
    for s in lines:
        greet((g, ahead[s]))
    pl.when(jnp.logical_not(first))(lambda: greet(before_id))
    pl.when(jnp.logical_not(last))(lambda: greet(after_id))

    lane = lax.broadcasted_iota(jnp.int32, (NVAR, LANES), 1)
    head = lane < CAP
    half = BAND * NVAR // 2
    packed = [jnp.zeros((NVAR, LANES), jnp.float32)] * 2
    loads[0].wait()
    for t in range(BAND * NVAR):
        tile = band_v[t // NVAR, t % NVAR].astype(jnp.float32)
        bandf[t] = tile
        start, end = tile[:, :LANES], tile[:, cells - LANES :]
        band_edge[t, :, :LANES] = end
        band_edge[t, :, 2 * LANES :] = start
        u = t % half
        ends = pltpu.roll(jnp.where(head, start, end), 8 * u + 4, 1)
        packed[t // half] = jnp.where(lane // 8 == u, ends, packed[t // half])
    rest = jnp.zeros((8 - NVAR, LANES), jnp.float32)
    halo_s[0] = jnp.concatenate([packed[0], rest], axis=0)
    halo_s[1] = jnp.concatenate([packed[1], rest], axis=0)
    for load in loads[1:4]:
        load.wait()
    adj, grad, pre = adj_v[...], grad_v[...], pre_v[...]
    ends = [
        jnp.where(head, v[:, :LANES], v[:, cells - LANES :]) for v in (adj, grad, pre)
    ]
    packed = jnp.where(
        (lane < 16) | (lane >= 112),
        ends[0],
        jnp.where(head, pltpu.roll(ends[1], 32, 1), pltpu.roll(ends[2], 80, 1)),
    )
    halo_s[2] = jnp.concatenate([packed, rest], axis=0)

    @pl.when(first)
    def _():
        halo_l[...] = jnp.zeros_like(halo_l)

    @pl.when(last)
    def _():
        halo_r[...] = jnp.zeros_like(halo_r)

    loads[4].wait()
    cell = cell_v[...]
    owner, local = cell // cells, cell % cells
    far = ((owner // X - y + Y) % Y) * X + (owner % X - x + X) % X
    slots = lax.broadcasted_iota(jnp.int32, (dom_count, faces), 0)
    reads = jnp.where(slots == far, 1.0, 0.0)
    earlier = lax.broadcasted_iota(jnp.int32, (faces, faces), 0)
    later = lax.broadcasted_iota(jnp.int32, (faces, faces), 1)
    upper = jnp.where(earlier < later, 1.0, 0.0).astype(jnp.bfloat16)
    reads_b = reads.astype(jnp.bfloat16)
    counts = jnp.dot(reads_b, upper, preferred_element_type=jnp.float32)
    rank = jnp.sum(reads * counts, axis=0, keepdims=True).astype(jnp.int32)
    entry = lax.broadcasted_iota(jnp.int32, (2 * CAP, faces), 0)
    wanted = jnp.where(
        entry < CAP, (local // LANES).astype(jnp.float32), (local % LANES).astype(jnp.float32)
    )
    wanted = jnp.where(entry % CAP == rank, wanted, 0.0).astype(jnp.bfloat16)
    requests = lax.dot_general(
        reads_b, wanted, (((1,), (1,)), ((), ())), preferred_element_type=jnp.float32
    ).astype(jnp.int32)
    req_own[...] = requests[:X]
    for dy in range(1, Y):
        req_s[SLOT[dy]] = requests[X * dy : X * dy + X]

    def send(source, landing, send_sem, recv_sem, target):
        pltpu.make_async_remote_copy(
            src_ref=source,
            dst_ref=landing,
            send_sem=send_sem,
            recv_sem=recv_sem,
            device_id=(g, target),
            device_id_type=MESH,
        ).start()

    def wait_all(ref, start, count, sem):
        some = ref.at[pl.ds(start, count)]
        pltpu.make_async_copy(some, some, sem).wait()

    inner = sweep(adj, grad, pre, bandf, shf, cells)
    psi = [inner[:, c * LANES : (c + 1) * LANES] for c in range(blocks)]
    spare = jnp.concatenate(psi[tiles:], axis=0)
    for c in range(tiles):
        part = slice(c * LANES, (c + 1) * LANES)
        psi_s[:, part] = jnp.concatenate([psi[c], spare[2 * c : 2 * c + 2]], axis=0)

    missing = first.astype(jnp.int32) + last.astype(jnp.int32)
    pl.semaphore_wait(barrier, len(lines) + 2 - missing)

    halo_copies = []
    for i, (target, landing) in enumerate(((after_id, halo_l), (before_id, halo_r))):
        halo_copies.append(
            pltpu.make_async_remote_copy(
                src_ref=halo_s,
                dst_ref=landing,
                send_sem=halo_send.at[i],
                recv_sem=halo_recv.at[i],
                device_id=target,
                device_id_type=MESH,
            )
        )
    pl.when(jnp.logical_not(last))(halo_copies[0].start)
    pl.when(jnp.logical_not(first))(halo_copies[1].start)

    for dx in (2, 1, 3):
        i = X - dx
        send(psi_s, psi_r.at[i], psi_send, psi_recv, ahead[dx])
    for dy in (4, 3, 5, 2, 6, 1, 7):
        i = SLOT[dy]
        send(req_s.at[i], req_r.at[i], req_send, req_recv, ahead[X * dy])

    pick = jnp.broadcast_to(rank, (8, faces)) + jnp.where(
        lax.broadcasted_iota(jnp.int32, (8, faces), 0) < 3, 0, CAP
    )
    far8 = jnp.broadcast_to(far, (8, faces))
    loads[5].wait()
    box = box_v[...]
    box_far = ((box // X - y + Y) % Y) * X + (box % X - x + X) % X
    feeds = slots == box_far
    at_start, at_end = local < HALO, local >= cells - HALO
    end_place = jnp.where(at_start, local + HALO, local - (cells - HALO))
    takes_end = lax.broadcasted_iota(jnp.int32, (16, faces), 0) == end_place
    reads_end = at_start | at_end

    pl.when(jnp.logical_not(first))(halo_copies[0].wait_recv)
    pl.when(jnp.logical_not(last))(halo_copies[1].wait_recv)
    left = halo_l[:, :NVAR, :]
    right = halo_r[:, :NVAR, :]
    from_left = lane % 8 < 4
    for h in range(2):
        both = jnp.where(from_left, left[h], right[h])
        for u in range(half):
            band_edge[h * half + u, :, LANES : 2 * LANES] = pltpu.roll(
                both, LANES - (8 * u + 4), 1
            )

    def edge(v, turn):
        between = jnp.where(head, right[2], left[2])
        if turn:
            between = jnp.where(
                head, pltpu.roll(right[2], turn, 1), pltpu.roll(left[2], turn, 1)
            )
        return jnp.concatenate(
            [v[:, cells - LANES :], between, v[:, :LANES]], axis=1
        )

    outer = sweep(
        edge(adj, 0), edge(grad, 96), edge(pre, 48), band_edge, shf, 3 * LANES
    )
    psi[0] = jnp.where(head, outer[:, 2 * LANES :], psi[0])
    psi[-1] = jnp.where(head, psi[-1], outer[:, :LANES])
    ends = jnp.where(head, psi[0], psi[-1])
    row = jnp.zeros((NVAR, LANES), jnp.float32)
    which = lax.broadcasted_iota(jnp.int32, (NVAR, LANES), 0)
    for v in range(NVAR):
        row = jnp.where(which == v, pltpu.roll(ends, 16 * v + HALO, 1), row)
    row = jnp.sum(jnp.where(lane // 16 == which, row, 0.0), axis=0, keepdims=True)
    ends_s[...] = row
    ends_r[0] = row
    wait_all(psi_r, 1, X - 1, psi_recv)
    for s in FAR_FIRST:
        back = (Y - s // X) % Y * X + (X - s % X) % X
        send(ends_s, ends_r.at[back], ends_send, ends_recv, ahead[s])
    for c in range(blocks):
        out_o[:NVAR, c * LANES : (c + 1) * LANES] = psi[c]
    out_o[NVAR:, :] = jnp.zeros((8 - NVAR, cells), jnp.float32)

    low8 = lax.broadcasted_iota(jnp.int32, (8, LANES), 1) < CAP
    low1 = low8[:1]

    def row_values(ref):
        parts = [ref[:, c * LANES : (c + 1) * LANES] for c in range(tiles)]
        size = 8 - NVAR
        for start in range(0, tiles, NVAR // size):
            some = [p[NVAR:] for p in parts[start : start + NVAR // size]]
            parts.append(jnp.concatenate(some + some[:1], axis=0))
        return parts

    def answers(values, wish, other):
        chunk = jnp.where(low1, wish, pltpu.roll(other, CAP, 1))
        place_in = jnp.where(low1, pltpu.roll(wish, CAP, 1), other)
        chunk = jnp.broadcast_to(chunk, (8, LANES))
        place_in = jnp.broadcast_to(place_in, (8, LANES))
        found = take_lanes(values[0], place_in)
        for c in range(1, blocks):
            found = jnp.where(chunk == c, take_lanes(values[c], place_in), found)
        turned = pltpu.roll(found, 5, 0)
        return (
            jnp.where(low8, found, pltpu.roll(turned, CAP, 1))[:3],
            jnp.where(low8, pltpu.roll(found, CAP, 1), turned)[:3],
        )

    pairs = ((4, 3), (5, 2), (6, 1), (7, 0))

    def answer(values, dx, pair):
        a, b = pair
        wish = req_r[SLOT[a], dx : dx + 1]
        other = req_r[SLOT[b], dx : dx + 1] if b else req_own[dx : dx + 1]
        one, two = answers(values, wish, other)
        resp_s[SLOT[a], 3 * dx : 3 * dx + 3] = one
        if b:
            resp_s[SLOT[b], 3 * dx : 3 * dx + 3] = two
        else:
            resp_own[3 * dx : 3 * dx + 3] = two

    wait_all(req_r, 0, Y - 1, req_recv)
    values = [row_values(psi_s)] + [row_values(psi_r.at[dx]) for dx in range(1, X)]
    for pair in pairs:
        for dx in range(X):
            answer(values[dx], dx, pair)
        for dy in pair:
            if dy:
                i = SLOT[dy]
                send(
                    resp_s.at[i],
                    resp_r.at[i],
                    resp_send,
                    resp_recv.at[0 if dy in NEAR else 1],
                    ahead[X * (Y - dy)],
                )

    found = [jnp.zeros((8, LANES), jnp.float32)] * (faces // LANES)

    def look(dy, ref):
        for dx in range(X):
            got = ref[3 * dx : 3 * dx + 3]
            got = jnp.concatenate([got, got, got[:2]], axis=0)
            for c in range(faces // LANES):
                part = slice(c * LANES, (c + 1) * LANES)
                found[c] = jnp.where(
                    far8[:, part] == dy * X + dx, take_lanes(got, pick[:, part]), found[c]
                )

    look(0, resp_own)
    wait_all(resp_r, 0, len(NEAR), resp_recv.at[0])
    for dy in NEAR:
        look(dy, resp_r.at[SLOT[dy]])
    loads[6].wait()
    wait_all(resp_r, len(NEAR), len(FAR), resp_recv.at[1])
    for dy in FAR:
        look(dy, resp_r.at[SLOT[dy]])
    face_psi = jnp.concatenate(found, axis=1)

    wait_all(ends_r, 1, dom_count - 1, ends_recv)
    ends = ends_r[...].reshape(dom_count, LANES)
    coarse = ends.astype(jnp.bfloat16)
    fine = (ends - coarse.astype(jnp.float32)).astype(jnp.bfloat16)
    picked = lax.dot_general(
        jnp.concatenate([coarse, fine], axis=0),
        jnp.concatenate([reads_b, reads_b], axis=0),
        (((0,), (0,)), ((), ())),
        preferred_element_type=jnp.float32,
    )
    sums = jnp.zeros((2 * dom_count, SENS), jnp.float32)
    for v in range(NVAR):
        end = jnp.where(takes_end, picked[16 * v : 16 * v + 16], 0.0)
        end = jnp.sum(end, axis=0, keepdims=True)
        value = jnp.where(reads_end, end, face_psi[v : v + 1])
        coarse = value.astype(jnp.bfloat16).astype(jnp.float32)
        fine = value - coarse
        weights = jnp.concatenate(
            [jnp.where(feeds, coarse, 0.0), jnp.where(feeds, fine, 0.0)], axis=0
        ).astype(jnp.bfloat16)
        sums = sums + jnp.dot(
            weights,
            jac_v[:, v * SENS : (v + 1) * SENS],
            preferred_element_type=jnp.float32,
        )
    sums = sums[:dom_count] + sums[dom_count:]
    for s in range(1, dom_count):
        part_s[s] = sums[s : s + 1]
    part_r[0] = sums[0:1]
    for s in FAR_FIRST:
        send(part_s.at[s], part_r.at[s], part_send, part_recv, ahead[s])
    wait_all(part_r, 1, dom_count - 1, part_recv)
    out_o[NVAR : NVAR + 1, :SENS] = jnp.sum(part_r[...], axis=0)
    pl.when(jnp.logical_not(last))(halo_copies[0].wait_send)
    pl.when(jnp.logical_not(first))(halo_copies[1].wait_send)
    wait_all(req_s, 0, Y - 1, req_send)
    wait_all(psi_r, 1, X - 1, psi_send)
    wait_all(resp_s, 0, Y - 1, resp_send)
    wait_all(ends_r, 1, dom_count - 1, ends_send)
    wait_all(part_s, 1, dom_count - 1, part_send)


def solution(mesh):
    groups = mesh.shape["group"]

    def shards(adjoint, gradient, precond, band, face_jac, face_cell, face_box):
        cells = adjoint.shape[1]
        faces = face_jac.shape[0]
        dom_count = X * Y
        packed = cells * NVAR // 8
        f32 = jnp.float32
        vmem = pltpu.VMEM
        dma = pltpu.SemaphoreType.DMA
        out = pl.pallas_call(
            functools.partial(kernel, groups),
            out_shape=vmem((8, cells), f32),
            in_specs=[pl.BlockSpec(memory_space=pl.ANY)] * 7,
            out_specs=pl.BlockSpec(memory_space=pltpu.VMEM),
            scratch_shapes=[
                vmem((NVAR, cells), f32),
                vmem((NVAR, cells), f32),
                vmem((NVAR, cells), f32),
                vmem((BAND, NVAR, NVAR, cells), jnp.bfloat16),
                vmem((faces, NVAR * SENS), jnp.bfloat16),
                vmem((1, faces), jnp.int32),
                vmem((1, faces), jnp.int32),
                vmem((BAND * NVAR, NVAR, cells), f32),
                vmem((BAND * NVAR, NVAR, 3 * LANES), f32),
                vmem((BAND, NVAR, cells), f32),
                vmem((3, 8, LANES), f32),
                vmem((3, 8, LANES), f32),
                vmem((3, 8, LANES), f32),
                vmem((8, packed), f32),
                vmem((X, 8, packed), f32),
                vmem((Y - 1, X, LANES), jnp.int32),
                vmem((Y - 1, X, LANES), jnp.int32),
                vmem((X, LANES), jnp.int32),
                vmem((Y - 1, 3 * X, LANES), f32),
                vmem((Y - 1, 3 * X, LANES), f32),
                vmem((3 * X, LANES), f32),
                vmem((1, LANES), f32),
                vmem((dom_count, 1, LANES), f32),
                vmem((dom_count, 1, LANES), f32),
                vmem((dom_count, 1, LANES), f32),
                dma((7,)),
                dma((2,)),
                dma((2,)),
                dma,
                dma,
                dma,
                dma,
                dma,
                dma((2,)),
                dma,
                dma,
                dma,
                dma,
            ],
            compiler_params=pltpu.CompilerParams(
                collective_id=0, has_side_effects=True
            ),
        )(
            adjoint,
            gradient,
            precond,
            band,
            face_jac,
            face_cell.reshape(1, faces),
            face_box.reshape(1, faces),
        )
        return out[:NVAR], out[NVAR : NVAR + 1, :SENS]

    return jax.shard_map(
        shards,
        mesh=mesh,
        in_specs=(
            P(None, ("group", "dom")),
            P(None, ("group", "dom")),
            P(None, ("group", "dom")),
            P(None, None, None, ("group", "dom")),
            P(("group", "dom"), None),
            P(("group", "dom")),
            P(("group", "dom"), None),
        ),
        out_specs=(P(None, ("group", "dom")), P(("group", "dom"), None)),
        check_vma=False,
    )
```

```python
import functools

import jax
import jax.numpy as jnp
from jax import lax
from jax.experimental import pallas as pl
from jax.experimental.pallas import tpu as pltpu
from jax.sharding import PartitionSpec as P

NVAR = 6
SENS = 128
BAND = 5
SWEEPS = 3
CAP = 64
HALO = 2 * SWEEPS
LANES = 128
X, Y = 4, 8
MESH = pl.DeviceIdType.MESH

FAR_FIRST = sorted(
    range(1, X * Y),
    key=lambda s: -(min(s % X, X - s % X) + min(s // X, Y - s // X)),
)
NEAR, FAR = (6, 7, 1, 2), (3, 4, 5)
SLOT = {dy: i for i, dy in enumerate(NEAR + FAR)}


def take_lanes(values, index):
    return jnp.take_along_axis(values, index, axis=1, mode="promise_in_bounds")


def sweep(psi, grad, pre, band_ref, shifted_ref, width):
    for _ in range(SWEEPS):
        for k in range(BAND):
            shifted_ref[k, :, :width] = (
                psi if k == 2 else pltpu.roll(psi, (2 - k) % width, 1)
            )
        sums = []
        for k in range(BAND):
            part = None
            for b in range(NVAR):
                column = jnp.broadcast_to(
                    shifted_ref[k, b : b + 1, :width], (NVAR, width)
                )
                term = band_ref[k * NVAR + b] * column
                part = term if part is None else part + term
            sums.append(part)
        total = (sums[0] + sums[1]) + (sums[2] + sums[3]) + sums[4]
        psi = psi + pre * (grad - total)
    return psi


def kernel(
    groups,
    adj_h,
    grad_h,
    pre_h,
    band_h,
    jac_h,
    cell_h,
    box_h,
    out_o,
    adj_v,
    grad_v,
    pre_v,
    band_v,
    jac_v,
    cell_v,
    box_v,
    bandf,
    band_edge,
    shf,
    halo_s,
    halo_l,
    halo_r,
    psi_s,
    psi_r,
    req_s,
    req_r,
    req_own,
    resp_s,
    resp_r,
    resp_own,
    ends_s,
    ends_r,
    part_s,
    part_r,
    in_sem,
    halo_send,
    halo_recv,
    told,
    psi_send,
    psi_recv,
    req_send,
    req_recv,
    resp_send,
    resp_recv,
    ends_send,
    ends_recv,
    part_send,
    part_recv,
):
    cells = adj_h.shape[1]
    faces = jac_h.shape[0]
    dom_count = X * Y
    blocks = cells // LANES
    tiles = blocks * NVAR // 8
    g = lax.axis_index("group")
    d = lax.axis_index("dom")
    y, x = d // X, d % X
    rows = [((y + dy) % Y) * X for dy in range(Y)]
    columns = [(x + dx) % X for dx in range(X)]
    ahead = [rows[s // X] + columns[s % X] for s in range(dom_count)]
    total = groups * dom_count
    place = g * dom_count + d
    after = (place + 1) % total
    before = (place + total - 1) % total
    after_id = (after // dom_count, after % dom_count)
    before_id = (before // dom_count, before % dom_count)
    first, last = place == 0, place == total - 1

    loads = [
        pltpu.make_async_copy(src, dst, in_sem.at[i])
        for i, (src, dst) in enumerate(
            (
                (band_h, band_v),
                (adj_h, adj_v),
                (grad_h, grad_v),
                (pre_h, pre_v),
                (cell_h, cell_v),
                (box_h, box_v),
                (jac_h, jac_v),
            )
        )
    ]
    for load in loads:
        load.start()

    barrier = pltpu.get_barrier_semaphore()

    def greet(target):
        pl.semaphore_signal(barrier, inc=1, device_id=target, device_id_type=MESH)

    lines = [X * dy for dy in (4, 3, 5, 2, 6, 1, 7)] + [2, 1, 3]
    for s in lines:
        greet((g, ahead[s]))
    pl.when(jnp.logical_not(first))(lambda: greet(before_id))
    pl.when(jnp.logical_not(last))(lambda: greet(after_id))

    lane = lax.broadcasted_iota(jnp.int32, (NVAR, LANES), 1)
    head = lane < CAP
    half = BAND * NVAR // 2
    packed = [jnp.zeros((NVAR, LANES), jnp.float32)] * 2
    loads[0].wait()
    for t in range(BAND * NVAR):
        tile = band_v[t // NVAR, t % NVAR].astype(jnp.float32)
        bandf[t] = tile
        start, end = tile[:, :LANES], tile[:, cells - LANES :]
        band_edge[t, :, :LANES] = end
        band_edge[t, :, 2 * LANES :] = start
        u = t % half
        ends = pltpu.roll(jnp.where(head, start, end), 8 * u + 4, 1)
        packed[t // half] = jnp.where(lane // 8 == u, ends, packed[t // half])
    rest = jnp.zeros((8 - NVAR, LANES), jnp.float32)
    halo_s[0] = jnp.concatenate([packed[0], rest], axis=0)
    halo_s[1] = jnp.concatenate([packed[1], rest], axis=0)
    for load in loads[1:4]:
        load.wait()
    adj, grad, pre = adj_v[...], grad_v[...], pre_v[...]
    ends = [
        jnp.where(head, v[:, :LANES], v[:, cells - LANES :]) for v in (adj, grad, pre)
    ]
    packed = jnp.where(
        (lane < 16) | (lane >= 112),
        ends[0],
        jnp.where(head, pltpu.roll(ends[1], 32, 1), pltpu.roll(ends[2], 80, 1)),
    )
    halo_s[2] = jnp.concatenate([packed, rest], axis=0)

    @pl.when(first)
    def _():
        halo_l[...] = jnp.zeros_like(halo_l)

    @pl.when(last)
    def _():
        halo_r[...] = jnp.zeros_like(halo_r)

    loads[4].wait()
    cell = cell_v[...]
    owner, local = cell // cells, cell % cells
    far = ((owner // X - y + Y) % Y) * X + (owner % X - x + X) % X
    slots = lax.broadcasted_iota(jnp.int32, (dom_count, faces), 0)
    reads = jnp.where(slots == far, 1.0, 0.0)
    earlier = lax.broadcasted_iota(jnp.int32, (faces, faces), 0)
    later = lax.broadcasted_iota(jnp.int32, (faces, faces), 1)
    upper = jnp.where(earlier < later, 1.0, 0.0).astype(jnp.bfloat16)
    reads_b = reads.astype(jnp.bfloat16)
    counts = jnp.dot(reads_b, upper, preferred_element_type=jnp.float32)
    rank = jnp.sum(reads * counts, axis=0, keepdims=True).astype(jnp.int32)
    entry = lax.broadcasted_iota(jnp.int32, (2 * CAP, faces), 0)
    wanted = jnp.where(
        entry < CAP, (local // LANES).astype(jnp.float32), (local % LANES).astype(jnp.float32)
    )
    wanted = jnp.where(entry % CAP == rank, wanted, 0.0).astype(jnp.bfloat16)
    requests = lax.dot_general(
        reads_b, wanted, (((1,), (1,)), ((), ())), preferred_element_type=jnp.float32
    ).astype(jnp.int32)
    req_own[...] = requests[:X]
    for dy in range(1, Y):
        req_s[SLOT[dy]] = requests[X * dy : X * dy + X]

    def send(source, landing, send_sem, recv_sem, target):
        pltpu.make_async_remote_copy(
            src_ref=source,
            dst_ref=landing,
            send_sem=send_sem,
            recv_sem=recv_sem,
            device_id=(g, target),
            device_id_type=MESH,
        ).start()

    def wait_all(ref, start, count, sem):
        some = ref.at[pl.ds(start, count)]
        pltpu.make_async_copy(some, some, sem).wait()

    inner = sweep(adj, grad, pre, bandf, shf, cells)
    psi = [inner[:, c * LANES : (c + 1) * LANES] for c in range(blocks)]
    spare = jnp.concatenate(psi[tiles:], axis=0)
    for c in range(tiles):
        part = slice(c * LANES, (c + 1) * LANES)
        psi_s[:, part] = jnp.concatenate([psi[c], spare[2 * c : 2 * c + 2]], axis=0)

    missing = first.astype(jnp.int32) + last.astype(jnp.int32)
    pl.semaphore_wait(barrier, len(lines) + 2 - missing)

    halo_copies = []
    for i, (target, landing) in enumerate(((after_id, halo_l), (before_id, halo_r))):
        halo_copies.append(
            pltpu.make_async_remote_copy(
                src_ref=halo_s,
                dst_ref=landing,
                send_sem=halo_send.at[i],
                recv_sem=halo_recv.at[i],
                device_id=target,
                device_id_type=MESH,
            )
        )
    pl.when(jnp.logical_not(last))(halo_copies[0].start)
    pl.when(jnp.logical_not(first))(halo_copies[1].start)

    for dx in (2, 1, 3):
        i = X - dx
        send(psi_s, psi_r.at[i], psi_send, psi_recv, ahead[dx])
    for dy in (4, 3, 5, 2, 6, 1, 7):
        i = SLOT[dy]
        send(req_s.at[i], req_r.at[i], req_send, req_recv, ahead[X * dy])
    for dx in (2, 1, 3):
        pl.semaphore_signal(
            told, inc=1, device_id=(g, ahead[dx]), device_id_type=MESH
        )

    pick = jnp.broadcast_to(rank, (8, faces)) + jnp.where(
        lax.broadcasted_iota(jnp.int32, (8, faces), 0) < 3, 0, CAP
    )
    far8 = jnp.broadcast_to(far, (8, faces))
    loads[5].wait()
    box = box_v[...]
    box_far = ((box // X - y + Y) % Y) * X + (box % X - x + X) % X
    feeds = slots == box_far
    at_start, at_end = local < HALO, local >= cells - HALO
    end_place = jnp.where(at_start, local + HALO, local - (cells - HALO))
    takes_end = lax.broadcasted_iota(jnp.int32, (16, faces), 0) == end_place
    reads_end = at_start | at_end

    low8 = lax.broadcasted_iota(jnp.int32, (8, LANES), 1) < CAP
    low1 = low8[:1]

    def row_values(ref):
        parts = [ref[:, c * LANES : (c + 1) * LANES] for c in range(tiles)]
        size = 8 - NVAR
        for start in range(0, tiles, NVAR // size):
            some = [p[NVAR:] for p in parts[start : start + NVAR // size]]
            parts.append(jnp.concatenate(some + some[:1], axis=0))
        return parts

    def answers(values, wish, other):
        chunk = jnp.where(low1, wish, pltpu.roll(other, CAP, 1))
        place_in = jnp.where(low1, pltpu.roll(wish, CAP, 1), other)
        chunk = jnp.broadcast_to(chunk, (8, LANES))
        place_in = jnp.broadcast_to(place_in, (8, LANES))
        found = take_lanes(values[0], place_in)
        for c in range(1, blocks):
            found = jnp.where(chunk == c, take_lanes(values[c], place_in), found)
        turned = pltpu.roll(found, 5, 0)
        return (
            jnp.where(low8, found, pltpu.roll(turned, CAP, 1))[:3],
            jnp.where(low8, pltpu.roll(found, CAP, 1), turned)[:3],
        )

    pairs = ((4, 3), (5, 2), (6, 1), (7, 0))

    def answer(values, dx, pair):
        a, b = pair
        wish = req_r[SLOT[a], dx : dx + 1]
        other = req_r[SLOT[b], dx : dx + 1] if b else req_own[dx : dx + 1]
        one, two = answers(values, wish, other)
        resp_s[SLOT[a], 3 * dx : 3 * dx + 3] = one
        if b:
            resp_s[SLOT[b], 3 * dx : 3 * dx + 3] = two
        else:
            resp_own[3 * dx : 3 * dx + 3] = two

    def answer_all():
        wait_all(psi_r, 1, X - 1, psi_recv)
        wait_all(req_r, 0, Y - 1, req_recv)
        values = [row_values(psi_s)] + [row_values(psi_r.at[dx]) for dx in range(1, X)]
        for pair in pairs:
            for dx in range(X):
                answer(values[dx], dx, pair)
            for dy in pair:
                if dy:
                    i = SLOT[dy]
                    send(
                        resp_s.at[i],
                        resp_r.at[i],
                        resp_send,
                        resp_recv.at[0 if dy in NEAR else 1],
                        ahead[X * (Y - dy)],
                    )

    waits = place == (Y // 2) * X - 1
    pl.when(waits)(answer_all)

    pl.when(jnp.logical_not(first))(halo_copies[0].wait_recv)
    pl.when(jnp.logical_not(last))(halo_copies[1].wait_recv)
    left = halo_l[:, :NVAR, :]
    right = halo_r[:, :NVAR, :]
    from_left = lane % 8 < 4
    for h in range(2):
        both = jnp.where(from_left, left[h], right[h])
        for u in range(half):
            band_edge[h * half + u, :, LANES : 2 * LANES] = pltpu.roll(
                both, LANES - (8 * u + 4), 1
            )

    def edge(v, turn):
        between = jnp.where(head, right[2], left[2])
        if turn:
            between = jnp.where(
                head, pltpu.roll(right[2], turn, 1), pltpu.roll(left[2], turn, 1)
            )
        return jnp.concatenate(
            [v[:, cells - LANES :], between, v[:, :LANES]], axis=1
        )

    outer = sweep(
        edge(adj, 0), edge(grad, 96), edge(pre, 48), band_edge, shf, 3 * LANES
    )
    psi[0] = jnp.where(head, outer[:, 2 * LANES :], psi[0])
    psi[-1] = jnp.where(head, psi[-1], outer[:, :LANES])
    ends = jnp.where(head, psi[0], psi[-1])
    row = jnp.zeros((NVAR, LANES), jnp.float32)
    which = lax.broadcasted_iota(jnp.int32, (NVAR, LANES), 0)
    for v in range(NVAR):
        row = jnp.where(which == v, pltpu.roll(ends, 16 * v + HALO, 1), row)
    row = jnp.sum(jnp.where(lane // 16 == which, row, 0.0), axis=0, keepdims=True)
    ends_s[...] = row
    ends_r[0] = row
    pl.semaphore_wait(told, X - 1)
    for s in FAR_FIRST:
        back = (Y - s // X) % Y * X + (X - s % X) % X
        send(ends_s, ends_r.at[back], ends_send, ends_recv, ahead[s])
    for c in range(blocks):
        out_o[:NVAR, c * LANES : (c + 1) * LANES] = psi[c]
    out_o[NVAR:, :] = jnp.zeros((8 - NVAR, cells), jnp.float32)

    pl.when(jnp.logical_not(waits))(answer_all)

    found = [jnp.zeros((8, LANES), jnp.float32)] * (faces // LANES)

    def look(dy, ref):
        for dx in range(X):
            got = ref[3 * dx : 3 * dx + 3]
            got = jnp.concatenate([got, got, got[:2]], axis=0)
            for c in range(faces // LANES):
                part = slice(c * LANES, (c + 1) * LANES)
                found[c] = jnp.where(
                    far8[:, part] == dy * X + dx, take_lanes(got, pick[:, part]), found[c]
                )

    look(0, resp_own)
    wait_all(resp_r, 0, len(NEAR), resp_recv.at[0])
    for dy in NEAR:
        look(dy, resp_r.at[SLOT[dy]])
    loads[6].wait()
    wait_all(resp_r, len(NEAR), len(FAR), resp_recv.at[1])
    for dy in FAR:
        look(dy, resp_r.at[SLOT[dy]])
    face_psi = jnp.concatenate(found, axis=1)

    wait_all(ends_r, 1, dom_count - 1, ends_recv)
    ends = ends_r[...].reshape(dom_count, LANES)
    coarse = ends.astype(jnp.bfloat16)
    fine = (ends - coarse.astype(jnp.float32)).astype(jnp.bfloat16)
    picked = lax.dot_general(
        jnp.concatenate([coarse, fine], axis=0),
        jnp.concatenate([reads_b, reads_b], axis=0),
        (((0,), (0,)), ((), ())),
        preferred_element_type=jnp.float32,
    )
    sums = jnp.zeros((2 * dom_count, SENS), jnp.float32)
    for v in range(NVAR):
        end = jnp.where(takes_end, picked[16 * v : 16 * v + 16], 0.0)
        end = jnp.sum(end, axis=0, keepdims=True)
        value = jnp.where(reads_end, end, face_psi[v : v + 1])
        coarse = value.astype(jnp.bfloat16).astype(jnp.float32)
        fine = value - coarse
        weights = jnp.concatenate(
            [jnp.where(feeds, coarse, 0.0), jnp.where(feeds, fine, 0.0)], axis=0
        ).astype(jnp.bfloat16)
        sums = sums + jnp.dot(
            weights,
            jac_v[:, v * SENS : (v + 1) * SENS],
            preferred_element_type=jnp.float32,
        )
    sums = sums[:dom_count] + sums[dom_count:]
    for s in range(1, dom_count):
        part_s[s] = sums[s : s + 1]
    part_r[0] = sums[0:1]
    for s in FAR_FIRST:
        send(part_s.at[s], part_r.at[s], part_send, part_recv, ahead[s])
    wait_all(part_r, 1, dom_count - 1, part_recv)
    out_o[NVAR : NVAR + 1, :SENS] = jnp.sum(part_r[...], axis=0)
    pl.when(jnp.logical_not(last))(halo_copies[0].wait_send)
    pl.when(jnp.logical_not(first))(halo_copies[1].wait_send)
    wait_all(req_s, 0, Y - 1, req_send)
    wait_all(psi_r, 1, X - 1, psi_send)
    wait_all(resp_s, 0, Y - 1, resp_send)
    wait_all(ends_r, 1, dom_count - 1, ends_send)
    wait_all(part_s, 1, dom_count - 1, part_send)


def solution(mesh):
    groups = mesh.shape["group"]

    def shards(adjoint, gradient, precond, band, face_jac, face_cell, face_box):
        cells = adjoint.shape[1]
        faces = face_jac.shape[0]
        dom_count = X * Y
        packed = cells * NVAR // 8
        f32 = jnp.float32
        vmem = pltpu.VMEM
        dma = pltpu.SemaphoreType.DMA
        out = pl.pallas_call(
            functools.partial(kernel, groups),
            out_shape=vmem((8, cells), f32),
            in_specs=[pl.BlockSpec(memory_space=pl.ANY)] * 7,
            out_specs=pl.BlockSpec(memory_space=pltpu.VMEM),
            scratch_shapes=[
                vmem((NVAR, cells), f32),
                vmem((NVAR, cells), f32),
                vmem((NVAR, cells), f32),
                vmem((BAND, NVAR, NVAR, cells), jnp.bfloat16),
                vmem((faces, NVAR * SENS), jnp.bfloat16),
                vmem((1, faces), jnp.int32),
                vmem((1, faces), jnp.int32),
                vmem((BAND * NVAR, NVAR, cells), f32),
                vmem((BAND * NVAR, NVAR, 3 * LANES), f32),
                vmem((BAND, NVAR, cells), f32),
                vmem((3, 8, LANES), f32),
                vmem((3, 8, LANES), f32),
                vmem((3, 8, LANES), f32),
                vmem((8, packed), f32),
                vmem((X, 8, packed), f32),
                vmem((Y - 1, X, LANES), jnp.int32),
                vmem((Y - 1, X, LANES), jnp.int32),
                vmem((X, LANES), jnp.int32),
                vmem((Y - 1, 3 * X, LANES), f32),
                vmem((Y - 1, 3 * X, LANES), f32),
                vmem((3 * X, LANES), f32),
                vmem((1, LANES), f32),
                vmem((dom_count, 1, LANES), f32),
                vmem((dom_count, 1, LANES), f32),
                vmem((dom_count, 1, LANES), f32),
                dma((7,)),
                dma((2,)),
                dma((2,)),
                pltpu.SemaphoreType.REGULAR,
                dma,
                dma,
                dma,
                dma,
                dma,
                dma((2,)),
                dma,
                dma,
                dma,
                dma,
            ],
            compiler_params=pltpu.CompilerParams(
                collective_id=0, has_side_effects=True
            ),
        )(
            adjoint,
            gradient,
            precond,
            band,
            face_jac,
            face_cell.reshape(1, faces),
            face_box.reshape(1, faces),
        )
        return out[:NVAR], out[NVAR : NVAR + 1, :SENS]

    return jax.shard_map(
        shards,
        mesh=mesh,
        in_specs=(
            P(None, ("group", "dom")),
            P(None, ("group", "dom")),
            P(None, ("group", "dom")),
            P(None, None, None, ("group", "dom")),
            P(("group", "dom"), None),
            P(("group", "dom")),
            P(("group", "dom"), None),
        ),
        out_specs=(P(None, ("group", "dom")), P(("group", "dom"), None)),
        check_vma=False,
    )
```

```python
import functools

import jax
import jax.numpy as jnp
from jax import lax
from jax.experimental import pallas as pl
from jax.experimental.pallas import tpu as pltpu
from jax.sharding import PartitionSpec as P

NVAR = 6
SENS = 128
BAND = 5
SWEEPS = 3
CAP = 64
HALO = 2 * SWEEPS
LANES = 128
X, Y = 4, 8
MESH = pl.DeviceIdType.MESH

FAR_FIRST = sorted(
    range(1, X * Y),
    key=lambda s: -(min(s % X, X - s % X) + min(s // X, Y - s // X)),
)
NEAR, FAR = (6, 7, 1, 2), (3, 4, 5)
SLOT = {dy: i for i, dy in enumerate(NEAR + FAR)}


def take_lanes(values, index):
    return jnp.take_along_axis(values, index, axis=1, mode="promise_in_bounds")


def sweep(psi, grad, pre, band_ref, shifted_ref, width):
    for _ in range(SWEEPS):
        for k in range(BAND):
            shifted_ref[k, :, :width] = (
                psi if k == 2 else pltpu.roll(psi, (2 - k) % width, 1)
            )
        sums = []
        for k in range(BAND):
            part = None
            for b in range(NVAR):
                column = jnp.broadcast_to(
                    shifted_ref[k, b : b + 1, :width], (NVAR, width)
                )
                term = band_ref[k * NVAR + b] * column
                part = term if part is None else part + term
            sums.append(part)
        total = (sums[0] + sums[1]) + (sums[2] + sums[3]) + sums[4]
        psi = psi + pre * (grad - total)
    return psi


def kernel(
    groups,
    adj_h,
    grad_h,
    pre_h,
    band_h,
    jac_h,
    cell_h,
    box_h,
    out_o,
    state_v,
    band_v,
    jac_v,
    face_v,
    bandf,
    band_edge,
    shf,
    halo_s,
    halo_l,
    halo_r,
    psi_s,
    psi_r,
    req_s,
    req_r,
    req_own,
    resp_s,
    resp_r,
    resp_own,
    ends_s,
    ends_r,
    part_s,
    part_r,
    count_v,
    in_sem,
    sent,
    halo_recv,
    told,
    psi_recv,
    req_recv,
    resp_send,
    resp_recv,
    ends_recv,
    part_recv,
):
    cells = adj_h.shape[1]
    faces = jac_h.shape[0]
    dom_count = X * Y
    blocks = cells // LANES
    tiles = blocks * NVAR // 8
    g = lax.axis_index("group")
    d = lax.axis_index("dom")
    y, x = d // X, d % X
    rows = [((y + dy) % Y) * X for dy in range(Y)]
    columns = [(x + dx) % X for dx in range(X)]
    ahead = [rows[s // X] + columns[s % X] for s in range(dom_count)]
    total = groups * dom_count
    place = g * dom_count + d
    after = (place + 1) % total
    before = (place + total - 1) % total
    after_id = (after // dom_count, after % dom_count)
    before_id = (before // dom_count, before % dom_count)
    first, last = place == 0, place == total - 1

    loads = [
        pltpu.make_async_copy(src, dst, in_sem.at[i])
        for src, dst, i in (
            (band_h, band_v, 0),
            (adj_h, state_v.at[0], 1),
            (grad_h, state_v.at[1], 1),
            (pre_h, state_v.at[2], 1),
            (cell_h, face_v.at[0], 2),
            (box_h, face_v.at[1], 2),
            (jac_h, jac_v, 3),
        )
    ]
    for load in loads:
        load.start()

    barrier = pltpu.get_barrier_semaphore()

    def greet(target):
        pl.semaphore_signal(barrier, inc=1, device_id=target, device_id_type=MESH)

    lines = [X * dy for dy in (4, 3, 5, 2, 6, 1, 7)] + [2, 1, 3]
    for s in lines:
        greet((g, ahead[s]))
    pl.when(jnp.logical_not(first))(lambda: greet(before_id))
    pl.when(jnp.logical_not(last))(lambda: greet(after_id))

    lane = lax.broadcasted_iota(jnp.int32, (NVAR, LANES), 1)
    head = lane < CAP
    half = BAND * NVAR // 2
    packed = [jnp.zeros((NVAR, LANES), jnp.float32)] * 2
    loads[0].wait()
    for t in range(BAND * NVAR):
        tile = band_v[t // NVAR, t % NVAR].astype(jnp.float32)
        bandf[t] = tile
        start, end = tile[:, :LANES], tile[:, cells - LANES :]
        turned = pltpu.roll(jnp.where(head, start, end), CAP, 1)
        band_edge[t, :, :LANES] = end
        band_edge[t, :, LANES:] = turned
        u = t % half
        ends = jnp.where(lane < 32, start, turned)
        ends = pltpu.roll(ends, 4 * u, 1) if u else ends
        own_lanes = (lane // 4 == u) | (lane // 4 == half + u)
        packed[t // half] = jnp.where(own_lanes, ends, packed[t // half])
    rest = jnp.zeros((8 - NVAR, LANES), jnp.float32)
    halo_s[0] = jnp.concatenate([packed[0], rest], axis=0)
    halo_s[1] = jnp.concatenate([packed[1], rest], axis=0)
    pltpu.make_async_copy(state_v, state_v, in_sem.at[1]).wait()
    adj, grad, pre = state_v[0], state_v[1], state_v[2]
    turned = [
        pltpu.roll(jnp.where(head, v[:, :LANES], v[:, cells - LANES :]), CAP, 1)
        for v in (adj, grad, pre)
    ]
    ends = [
        jnp.where(lane < 32, v[:, :LANES], t) for v, t in zip((adj, grad, pre), turned)
    ]
    packed = jnp.where(
        (lane < 16) | ((lane >= 48) & (lane < 72)),
        ends[0],
        jnp.where(
            (lane < 32) | ((lane >= 72) & (lane < 88)),
            pltpu.roll(ends[1], 16, 1),
            pltpu.roll(ends[2], 32, 1),
        ),
    )
    halo_s[2] = jnp.concatenate([packed, rest], axis=0)

    @pl.when(first)
    def _():
        halo_l[...] = jnp.zeros_like(halo_l)

    @pl.when(last)
    def _():
        halo_r[...] = jnp.zeros_like(halo_r)

    pltpu.make_async_copy(face_v, face_v, in_sem.at[2]).wait()
    cell = face_v[0]
    owner, local = cell // cells, cell % cells
    far = ((owner // X - y + Y) % Y) * X + (owner % X - x + X) % X
    slots = lax.broadcasted_iota(jnp.int32, (dom_count, faces), 0)
    reads = jnp.where(slots == far, 1.0, 0.0)
    earlier = lax.broadcasted_iota(jnp.int32, (faces, faces), 0)
    later = lax.broadcasted_iota(jnp.int32, (faces, faces), 1)
    upper = jnp.where(earlier < later, 1.0, 0.0).astype(jnp.bfloat16)
    reads_b = reads.astype(jnp.bfloat16)
    counts = jnp.dot(reads_b, upper, preferred_element_type=jnp.float32)
    rank = jnp.sum(reads * counts, axis=0, keepdims=True).astype(jnp.int32)
    entry = lax.broadcasted_iota(jnp.int32, (2 * CAP, faces), 0)
    wanted = jnp.where(
        entry < CAP, (local // LANES).astype(jnp.float32), (local % LANES).astype(jnp.float32)
    )
    wanted = jnp.where(entry % CAP == rank, wanted, 0.0).astype(jnp.bfloat16)
    requests = lax.dot_general(
        reads_b, wanted, (((1,), (1,)), ((), ())), preferred_element_type=jnp.float32
    ).astype(jnp.int32)
    req_own[...] = requests[:X]
    for dy in range(1, Y):
        req_s[SLOT[dy]] = requests[X * dy : X * dy + X]

    def send(source, landing, send_sem, recv_sem, target):
        pltpu.make_async_remote_copy(
            src_ref=source,
            dst_ref=landing,
            send_sem=send_sem,
            recv_sem=recv_sem,
            device_id=(g, target),
            device_id_type=MESH,
        ).start()

    def wait_all(ref, start, count, sem):
        some = ref.at[pl.ds(start, count)]
        pltpu.make_async_copy(some, some, sem).wait()

    inner = sweep(adj, grad, pre, bandf, shf, cells)
    psi = [inner[:, c * LANES : (c + 1) * LANES] for c in range(blocks)]
    spare = jnp.concatenate(psi[tiles:], axis=0)
    for c in range(tiles):
        part = slice(c * LANES, (c + 1) * LANES)
        psi_s[:, part] = jnp.concatenate([psi[c], spare[2 * c : 2 * c + 2]], axis=0)

    missing = first.astype(jnp.int32) + last.astype(jnp.int32)
    pl.semaphore_wait(barrier, len(lines) + 2 - missing)

    halo_copies = []
    for i, (target, landing) in enumerate(((after_id, halo_l), (before_id, halo_r))):
        halo_copies.append(
            pltpu.make_async_remote_copy(
                src_ref=halo_s,
                dst_ref=landing,
                send_sem=sent,
                recv_sem=halo_recv.at[i],
                device_id=target,
                device_id_type=MESH,
            )
        )
    pl.when(jnp.logical_not(last))(halo_copies[0].start)
    pl.when(jnp.logical_not(first))(halo_copies[1].start)

    for dx in (2, 1, 3):
        i = X - dx
        send(psi_s, psi_r.at[i], sent, psi_recv, ahead[dx])
    for dy in (4, 3, 5, 2, 6, 1, 7):
        i = SLOT[dy]
        send(req_s.at[i], req_r.at[i], sent, req_recv, ahead[X * dy])
    for dx in (2, 1, 3):
        pl.semaphore_signal(
            told, inc=1, device_id=(g, ahead[dx]), device_id_type=MESH
        )

    pick = jnp.broadcast_to(rank, (8, faces)) + jnp.where(
        lax.broadcasted_iota(jnp.int32, (8, faces), 0) < 3, 0, CAP
    )
    far8 = jnp.broadcast_to(far, (8, faces))
    box = face_v[1]
    box_far = ((box // X - y + Y) % Y) * X + (box % X - x + X) % X
    feeds = slots == box_far
    at_start, at_end = local < HALO, local >= cells - HALO
    end_place = jnp.where(at_start, local + HALO, local - (cells - HALO))
    takes_end = lax.broadcasted_iota(jnp.int32, (16, faces), 0) == end_place
    reads_end = at_start | at_end

    low8 = lax.broadcasted_iota(jnp.int32, (8, LANES), 1) < CAP
    low1 = low8[:1]

    def row_values(ref):
        parts = [ref[:, c * LANES : (c + 1) * LANES] for c in range(tiles)]
        size = 8 - NVAR
        for start in range(0, tiles, NVAR // size):
            some = [p[NVAR:] for p in parts[start : start + NVAR // size]]
            parts.append(jnp.concatenate(some + some[:1], axis=0))
        return parts

    def answers(values, wish, other):
        chunk = jnp.where(low1, wish, pltpu.roll(other, CAP, 1))
        place_in = jnp.where(low1, pltpu.roll(wish, CAP, 1), other)
        chunk = jnp.broadcast_to(chunk, (8, LANES))
        place_in = jnp.broadcast_to(place_in, (8, LANES))
        found = take_lanes(values[0], place_in)
        for c in range(1, blocks):
            found = jnp.where(chunk == c, take_lanes(values[c], place_in), found)
        turned = pltpu.roll(found, 5, 0)
        return (
            jnp.where(low8, found, pltpu.roll(turned, CAP, 1))[:3],
            jnp.where(low8, pltpu.roll(found, CAP, 1), turned)[:3],
        )

    pairs = ((4, 3), (5, 2), (6, 1), (7, 0))

    def answer(values, dx, pair):
        a, b = pair
        wish = req_r[SLOT[a], dx : dx + 1]
        other = req_r[SLOT[b], dx : dx + 1] if b else req_own[dx : dx + 1]
        one, two = answers(values, wish, other)
        resp_s[SLOT[a], 3 * dx : 3 * dx + 3] = one
        if b:
            resp_s[SLOT[b], 3 * dx : 3 * dx + 3] = two
        else:
            resp_own[3 * dx : 3 * dx + 3] = two

    def answer_all():
        wait_all(psi_r, 1, X - 1, psi_recv)
        wait_all(req_r, 0, Y - 1, req_recv)
        values = [row_values(psi_s)] + [row_values(psi_r.at[dx]) for dx in range(1, X)]
        for pair in pairs:
            for dx in range(X):
                answer(values[dx], dx, pair)
            for dy in pair:
                if dy:
                    i = SLOT[dy]
                    send(
                        resp_s.at[i],
                        resp_r.at[i],
                        resp_send,
                        resp_recv.at[0 if dy in NEAR else 1],
                        ahead[X * (Y - dy)],
                    )

    waits = place == (Y // 2) * X - 1
    pl.when(waits)(answer_all)

    pl.when(jnp.logical_not(first))(halo_copies[0].wait_recv)
    pl.when(jnp.logical_not(last))(halo_copies[1].wait_recv)
    left = halo_l[:, :NVAR, :]
    right = halo_r[:, :NVAR, :]
    for h in range(2):
        both = jnp.where(lane < 4 * half, right[h], left[h])
        for u in range(half):
            back = pltpu.roll(both, LANES - 4 * u, 1) if u else both
            band_edge[h * half + u, :, LANES : LANES + CAP] = back[:, :CAP]
    both = jnp.where(lane < 48, right[2], left[2])

    def edge(i, v):
        back = pltpu.roll(both, LANES - 16 * i, 1) if i else both
        middle = jnp.where(head, back, turned[i])
        return jnp.concatenate([v[:, cells - LANES :], middle], axis=1)

    outer = sweep(
        edge(0, adj), edge(1, grad), edge(2, pre), band_edge, shf, 2 * LANES
    )
    psi[0] = jnp.where(lane < 32, pltpu.roll(outer[:, LANES:], CAP, 1), psi[0])
    psi[-1] = jnp.where(head, psi[-1], outer[:, :LANES])
    ends = jnp.where(head, psi[0], psi[-1])
    row = jnp.zeros((NVAR, LANES), jnp.float32)
    which = lax.broadcasted_iota(jnp.int32, (NVAR, LANES), 0)
    for v in range(NVAR):
        row = jnp.where(which == v, pltpu.roll(ends, 16 * v + HALO, 1), row)
    row = jnp.sum(jnp.where(lane // 16 == which, row, 0.0), axis=0, keepdims=True)
    ends_s[...] = row
    ends_r[0] = row
    pl.semaphore_wait(told, X - 1)
    for s in FAR_FIRST:
        back = (Y - s // X) % Y * X + (X - s % X) % X
        send(ends_s, ends_r.at[back], sent, ends_recv, ahead[s])
    for c in range(blocks):
        out_o[:NVAR, c * LANES : (c + 1) * LANES] = psi[c]
    out_o[NVAR:, :] = jnp.zeros((8 - NVAR, cells), jnp.float32)

    pl.when(jnp.logical_not(waits))(answer_all)

    found = [jnp.zeros((8, LANES), jnp.float32)] * (faces // LANES)

    def look(dy, ref):
        for dx in range(X):
            got = ref[3 * dx : 3 * dx + 3]
            got = jnp.concatenate([got, got, got[:2]], axis=0)
            for c in range(faces // LANES):
                part = slice(c * LANES, (c + 1) * LANES)
                found[c] = jnp.where(
                    far8[:, part] == dy * X + dx, take_lanes(got, pick[:, part]), found[c]
                )

    look(0, resp_own)
    wait_all(resp_r, 0, len(NEAR), resp_recv.at[0])
    for dy in NEAR:
        look(dy, resp_r.at[SLOT[dy]])
    loads[6].wait()
    wait_all(resp_r, len(NEAR), len(FAR), resp_recv.at[1])
    for dy in FAR:
        look(dy, resp_r.at[SLOT[dy]])
    face_psi = jnp.concatenate(found, axis=1)

    wait_all(ends_r, 1, dom_count - 1, ends_recv)
    ends = ends_r[...].reshape(dom_count, LANES)
    coarse = ends.astype(jnp.bfloat16)
    fine = (ends - coarse.astype(jnp.float32)).astype(jnp.bfloat16)
    picked = lax.dot_general(
        jnp.concatenate([coarse, fine], axis=0),
        jnp.concatenate([reads_b, reads_b], axis=0),
        (((0,), (0,)), ((), ())),
        preferred_element_type=jnp.float32,
    )
    sums = jnp.zeros((2 * dom_count, SENS), jnp.float32)
    for v in range(NVAR):
        end = jnp.where(takes_end, picked[16 * v : 16 * v + 16], 0.0)
        end = jnp.sum(end, axis=0, keepdims=True)
        value = jnp.where(reads_end, end, face_psi[v : v + 1])
        coarse = value.astype(jnp.bfloat16).astype(jnp.float32)
        fine = value - coarse
        weights = jnp.concatenate(
            [jnp.where(feeds, coarse, 0.0), jnp.where(feeds, fine, 0.0)], axis=0
        ).astype(jnp.bfloat16)
        sums = sums + jnp.dot(
            weights,
            jac_v[:, v * SENS : (v + 1) * SENS],
            preferred_element_type=jnp.float32,
        )
    sums = sums[:dom_count] + sums[dom_count:]
    for s in range(1, dom_count):
        part_s[s] = sums[s : s + 1]
    part_r[0] = sums[0:1]
    for s in FAR_FIRST:
        send(part_s.at[s], part_r.at[s], sent, part_recv, ahead[s])
    wait_all(part_r, 1, dom_count - 1, part_recv)
    out_o[NVAR : NVAR + 1, :SENS] = jnp.sum(part_r[...], axis=0)
    wait_all(resp_s, 0, Y - 1, resp_send)
    left_rows = X * (Y - 1) + (X - 1) * 8 * tiles + 2 * (dom_count - 1)
    one_halo = jnp.logical_or(first, last)
    pl.when(one_halo)(lambda: wait_all(count_v, 0, left_rows + 24, sent))
    pl.when(jnp.logical_not(one_halo))(lambda: wait_all(count_v, 0, left_rows + 48, sent))


def solution(mesh):
    groups = mesh.shape["group"]

    def shards(adjoint, gradient, precond, band, face_jac, face_cell, face_box):
        cells = adjoint.shape[1]
        faces = face_jac.shape[0]
        dom_count = X * Y
        packed = cells * NVAR // 8
        f32 = jnp.float32
        vmem = pltpu.VMEM
        dma = pltpu.SemaphoreType.DMA
        out = pl.pallas_call(
            functools.partial(kernel, groups),
            out_shape=vmem((8, cells), f32),
            in_specs=[pl.BlockSpec(memory_space=pl.ANY)] * 7,
            out_specs=pl.BlockSpec(memory_space=pltpu.VMEM),
            scratch_shapes=[
                vmem((3, NVAR, cells), f32),
                vmem((BAND, NVAR, NVAR, cells), jnp.bfloat16),
                vmem((faces, NVAR * SENS), jnp.bfloat16),
                vmem((2, 1, faces), jnp.int32),
                vmem((BAND * NVAR, NVAR, cells), f32),
                vmem((BAND * NVAR, NVAR, 2 * LANES), f32),
                vmem((BAND, NVAR, cells), f32),
                vmem((3, 8, LANES), f32),
                vmem((3, 8, LANES), f32),
                vmem((3, 8, LANES), f32),
                vmem((8, packed), f32),
                vmem((X, 8, packed), f32),
                vmem((Y - 1, X, LANES), jnp.int32),
                vmem((Y - 1, X, LANES), jnp.int32),
                vmem((X, LANES), jnp.int32),
                vmem((Y - 1, 3 * X, LANES), f32),
                vmem((Y - 1, 3 * X, LANES), f32),
                vmem((3 * X, LANES), f32),
                vmem((1, LANES), f32),
                vmem((dom_count, 1, LANES), f32),
                vmem((dom_count, 1, LANES), f32),
                vmem((dom_count, 1, LANES), f32),
                vmem((X * (Y - 1) + 3 * packed * 8 // LANES + 2 * dom_count + 46, 1, LANES), f32),
                dma((4,)),
                dma,
                dma((2,)),
                pltpu.SemaphoreType.REGULAR,
                dma,
                dma,
                dma,
                dma((2,)),
                dma,
                dma,
            ],
            compiler_params=pltpu.CompilerParams(
                collective_id=0, has_side_effects=True
            ),
        )(
            adjoint,
            gradient,
            precond,
            band,
            face_jac,
            face_cell.reshape(1, faces),
            face_box.reshape(1, faces),
        )
        return out[:NVAR], out[NVAR : NVAR + 1, :SENS]

    return jax.shard_map(
        shards,
        mesh=mesh,
        in_specs=(
            P(None, ("group", "dom")),
            P(None, ("group", "dom")),
            P(None, ("group", "dom")),
            P(None, None, None, ("group", "dom")),
            P(("group", "dom"), None),
            P(("group", "dom")),
            P(("group", "dom"), None),
        ),
        out_specs=(P(None, ("group", "dom")), P(("group", "dom"), None)),
        check_vma=False,
    )
```

```python
import functools

import jax
import jax.numpy as jnp
from jax import lax
from jax.experimental import pallas as pl
from jax.experimental.pallas import tpu as pltpu
from jax.sharding import PartitionSpec as P

NVAR = 6
SENS = 128
BAND = 5
SWEEPS = 3
CAP = 64
HALO = 2 * SWEEPS
LANES = 128
X, Y = 4, 8
MESH = pl.DeviceIdType.MESH

FAR_FIRST = sorted(
    range(1, X * Y),
    key=lambda s: -(min(s % X, X - s % X) + min(s // X, Y - s // X)),
)
NEAR, FAR = (6, 7, 1, 2), (3, 4, 5)
SLOT = {dy: i for i, dy in enumerate(NEAR + FAR)}


def take_lanes(values, index):
    return jnp.take_along_axis(values, index, axis=1, mode="promise_in_bounds")


def sweep(psi, grad, pre, band_ref, shifted_ref, width):
    for _ in range(SWEEPS):
        for k in range(BAND):
            shifted_ref[k, :, :width] = (
                psi if k == 2 else pltpu.roll(psi, (2 - k) % width, 1)
            )
        sums = []
        for k in range(BAND):
            part = None
            for b in range(NVAR):
                column = jnp.broadcast_to(
                    shifted_ref[k, b : b + 1, :width], (NVAR, width)
                )
                term = band_ref[k * NVAR + b] * column
                part = term if part is None else part + term
            sums.append(part)
        total = (sums[0] + sums[1]) + (sums[2] + sums[3]) + sums[4]
        psi = psi + pre * (grad - total)
    return psi


def kernel(
    groups,
    adj_h,
    grad_h,
    pre_h,
    band_h,
    jac_h,
    cell_h,
    box_h,
    out_o,
    zero_o,
    state_v,
    band_v,
    jac_v,
    face_v,
    bandf,
    band_edge,
    shf,
    halo_s,
    halo_l,
    halo_r,
    psi_s,
    psi_r,
    req_s,
    req_r,
    req_own,
    resp_s,
    resp_r,
    resp_own,
    ends_s,
    ends_r,
    part_s,
    part_r,
    count_v,
    in_sem,
    sent,
    halo_recv,
    told,
    psi_recv,
    req_recv,
    resp_send,
    resp_recv,
    ends_recv,
    part_recv,
):
    cells = adj_h.shape[1]
    faces = jac_h.shape[0]
    dom_count = X * Y
    blocks = cells // LANES
    tiles = blocks * NVAR // 8
    g = lax.axis_index("group")
    d = lax.axis_index("dom")
    y, x = d // X, d % X
    rows = [((y + dy) % Y) * X for dy in range(Y)]
    columns = [(x + dx) % X for dx in range(X)]
    ahead = [rows[s // X] + columns[s % X] for s in range(dom_count)]
    total = groups * dom_count
    place = g * dom_count + d
    after = (place + 1) % total
    before = (place + total - 1) % total
    after_id = (after // dom_count, after % dom_count)
    before_id = (before // dom_count, before % dom_count)
    first, last = place == 0, place == total - 1

    loads = [
        pltpu.make_async_copy(src, dst, in_sem.at[i])
        for src, dst, i in (
            (band_h, band_v, 0),
            (adj_h, state_v.at[0], 1),
            (grad_h, state_v.at[1], 1),
            (pre_h, state_v.at[2], 1),
            (cell_h, face_v.at[0], 2),
            (box_h, face_v.at[1], 2),
            (jac_h, jac_v, 3),
        )
    ]
    for load in loads:
        load.start()

    barrier = pltpu.get_barrier_semaphore()

    def greet(target):
        pl.semaphore_signal(barrier, inc=1, device_id=target, device_id_type=MESH)

    lines = [X * dy for dy in (4, 3, 5, 2, 6, 1, 7)] + [2, 1, 3]
    for s in lines:
        greet((g, ahead[s]))
    pl.when(jnp.logical_not(first))(lambda: greet(before_id))
    pl.when(jnp.logical_not(last))(lambda: greet(after_id))

    lane = lax.broadcasted_iota(jnp.int32, (NVAR, LANES), 1)
    head = lane < CAP
    half = BAND * NVAR // 2
    packed = [jnp.zeros((NVAR, LANES), jnp.float32)] * 2
    loads[0].wait()
    for t in range(BAND * NVAR):
        tile = band_v[t // NVAR, t % NVAR].astype(jnp.float32)
        bandf[t] = tile
        start, end = tile[:, :LANES], tile[:, cells - LANES :]
        turned = pltpu.roll(jnp.where(head, start, end), CAP, 1)
        band_edge[t, :, :LANES] = end
        band_edge[t, :, LANES:] = turned
        u = t % half
        ends = jnp.where(lane < 32, start, turned)
        ends = pltpu.roll(ends, 4 * u, 1) if u else ends
        own_lanes = (lane // 4 == u) | (lane // 4 == half + u)
        packed[t // half] = jnp.where(own_lanes, ends, packed[t // half])
    rest = jnp.zeros((8 - NVAR, LANES), jnp.float32)
    halo_s[0] = jnp.concatenate([packed[0], rest], axis=0)
    halo_s[1] = jnp.concatenate([packed[1], rest], axis=0)
    pltpu.make_async_copy(state_v, state_v, in_sem.at[1]).wait()
    adj, grad, pre = state_v[0], state_v[1], state_v[2]
    turned = [
        pltpu.roll(jnp.where(head, v[:, :LANES], v[:, cells - LANES :]), CAP, 1)
        for v in (adj, grad, pre)
    ]
    ends = [
        jnp.where(lane < 32, v[:, :LANES], t) for v, t in zip((adj, grad, pre), turned)
    ]
    packed = jnp.where(
        (lane < 16) | ((lane >= 48) & (lane < 72)),
        ends[0],
        jnp.where(
            (lane < 32) | ((lane >= 72) & (lane < 88)),
            pltpu.roll(ends[1], 16, 1),
            pltpu.roll(ends[2], 32, 1),
        ),
    )
    halo_s[2] = jnp.concatenate([packed, rest], axis=0)

    @pl.when(first)
    def _():
        halo_l[...] = jnp.zeros_like(halo_l)

    @pl.when(last)
    def _():
        halo_r[...] = jnp.zeros_like(halo_r)

    pltpu.make_async_copy(face_v, face_v, in_sem.at[2]).wait()
    cell = face_v[0]
    owner, local = cell // cells, cell % cells
    far = ((owner // X - y + Y) % Y) * X + (owner % X - x + X) % X
    slots = lax.broadcasted_iota(jnp.int32, (dom_count, faces), 0)
    reads = jnp.where(slots == far, 1.0, 0.0)
    earlier = lax.broadcasted_iota(jnp.int32, (faces, faces), 0)
    later = lax.broadcasted_iota(jnp.int32, (faces, faces), 1)
    upper = jnp.where(earlier < later, 1.0, 0.0).astype(jnp.bfloat16)
    reads_b = reads.astype(jnp.bfloat16)
    counts = jnp.dot(reads_b, upper, preferred_element_type=jnp.float32)
    rank = jnp.sum(reads * counts, axis=0, keepdims=True).astype(jnp.int32)
    entry = lax.broadcasted_iota(jnp.int32, (2 * CAP, faces), 0)
    wanted = jnp.where(
        entry < CAP, (local // LANES).astype(jnp.float32), (local % LANES).astype(jnp.float32)
    )
    wanted = jnp.where(entry % CAP == rank, wanted, 0.0).astype(jnp.bfloat16)
    requests = lax.dot_general(
        reads_b, wanted, (((1,), (1,)), ((), ())), preferred_element_type=jnp.float32
    ).astype(jnp.int32)
    req_own[...] = requests[:X]
    for dy in range(1, Y):
        req_s[SLOT[dy]] = requests[X * dy : X * dy + X]

    def send(source, landing, send_sem, recv_sem, target):
        pltpu.make_async_remote_copy(
            src_ref=source,
            dst_ref=landing,
            send_sem=send_sem,
            recv_sem=recv_sem,
            device_id=(g, target),
            device_id_type=MESH,
        ).start()

    def wait_all(ref, start, count, sem):
        some = ref.at[pl.ds(start, count)]
        pltpu.make_async_copy(some, some, sem).wait()

    inner = sweep(adj, grad, pre, bandf, shf, cells)
    psi = [inner[:, c * LANES : (c + 1) * LANES] for c in range(blocks)]
    spare = jnp.concatenate(psi[tiles:], axis=0)
    for c in range(tiles):
        part = slice(c * LANES, (c + 1) * LANES)
        psi_s[:, part] = jnp.concatenate([psi[c], spare[2 * c : 2 * c + 2]], axis=0)

    missing = first.astype(jnp.int32) + last.astype(jnp.int32)
    pl.semaphore_wait(barrier, len(lines) + 2 - missing)

    halo_copies = []
    for i, (target, landing) in enumerate(((after_id, halo_l), (before_id, halo_r))):
        halo_copies.append(
            pltpu.make_async_remote_copy(
                src_ref=halo_s,
                dst_ref=landing,
                send_sem=sent,
                recv_sem=halo_recv.at[i],
                device_id=target,
                device_id_type=MESH,
            )
        )
    pl.when(jnp.logical_not(last))(halo_copies[0].start)
    pl.when(jnp.logical_not(first))(halo_copies[1].start)

    for dx in (2, 1, 3):
        i = X - dx
        send(psi_s, psi_r.at[i], sent, psi_recv, ahead[dx])
    for dy in (4, 3, 5, 2, 6, 1, 7):
        i = SLOT[dy]
        send(req_s.at[i], req_r.at[i], sent, req_recv, ahead[X * dy])
    for dx in (2, 1, 3):
        pl.semaphore_signal(
            told, inc=1, device_id=(g, ahead[dx]), device_id_type=MESH
        )

    pick = jnp.broadcast_to(rank, (8, faces)) + jnp.where(
        lax.broadcasted_iota(jnp.int32, (8, faces), 0) < 3, 0, CAP
    )
    far8 = jnp.broadcast_to(far, (8, faces))
    box = face_v[1]
    box_far = ((box // X - y + Y) % Y) * X + (box % X - x + X) % X
    feeds = slots == box_far
    at_start, at_end = local < HALO, local >= cells - HALO
    end_place = jnp.where(at_start, local + HALO, local - (cells - HALO))
    takes_end = lax.broadcasted_iota(jnp.int32, (16, faces), 0) == end_place
    reads_end = at_start | at_end

    low8 = lax.broadcasted_iota(jnp.int32, (8, LANES), 1) < CAP
    low1 = low8[:1]

    def row_values(ref):
        parts = [ref[:, c * LANES : (c + 1) * LANES] for c in range(tiles)]
        size = 8 - NVAR
        for start in range(0, tiles, NVAR // size):
            some = [p[NVAR:] for p in parts[start : start + NVAR // size]]
            parts.append(jnp.concatenate(some + some[:1], axis=0))
        return parts

    def answers(values, wish, other):
        chunk = jnp.where(low1, wish, pltpu.roll(other, CAP, 1))
        place_in = jnp.where(low1, pltpu.roll(wish, CAP, 1), other)
        chunk = jnp.broadcast_to(chunk, (8, LANES))
        place_in = jnp.broadcast_to(place_in, (8, LANES))
        found = take_lanes(values[0], place_in)
        for c in range(1, blocks):
            found = jnp.where(chunk == c, take_lanes(values[c], place_in), found)
        turned = pltpu.roll(found, 5, 0)
        return (
            jnp.where(low8, found, pltpu.roll(turned, CAP, 1))[:3],
            jnp.where(low8, pltpu.roll(found, CAP, 1), turned)[:3],
        )

    pairs = ((4, 3), (5, 2), (6, 1), (7, 0))

    def answer(values, dx, pair):
        a, b = pair
        wish = req_r[SLOT[a], dx : dx + 1]
        other = req_r[SLOT[b], dx : dx + 1] if b else req_own[dx : dx + 1]
        one, two = answers(values, wish, other)
        resp_s[SLOT[a], 3 * dx : 3 * dx + 3] = one
        if b:
            resp_s[SLOT[b], 3 * dx : 3 * dx + 3] = two
        else:
            resp_own[3 * dx : 3 * dx + 3] = two

    def answer_all():
        wait_all(psi_r, 1, X - 1, psi_recv)
        wait_all(req_r, 0, Y - 1, req_recv)
        values = [row_values(psi_s)] + [row_values(psi_r.at[dx]) for dx in range(1, X)]
        for pair in pairs:
            for dx in range(X):
                answer(values[dx], dx, pair)
            for dy in pair:
                if dy:
                    i = SLOT[dy]
                    send(
                        resp_s.at[i],
                        resp_r.at[i],
                        resp_send,
                        resp_recv.at[0 if dy in NEAR else 1],
                        ahead[X * (Y - dy)],
                    )

    waits = place == (Y // 2) * X - 1
    pl.when(waits)(answer_all)

    pl.when(jnp.logical_not(first))(halo_copies[0].wait_recv)
    pl.when(jnp.logical_not(last))(halo_copies[1].wait_recv)
    left = halo_l[:, :NVAR, :]
    right = halo_r[:, :NVAR, :]
    for h in range(2):
        both = jnp.where(lane < 4 * half, right[h], left[h])
        for u in range(half):
            back = pltpu.roll(both, LANES - 4 * u, 1) if u else both
            band_edge[h * half + u, :, LANES : LANES + CAP] = back[:, :CAP]
    both = jnp.where(lane < 48, right[2], left[2])

    def edge(i, v):
        back = pltpu.roll(both, LANES - 16 * i, 1) if i else both
        middle = jnp.where(head, back, turned[i])
        return jnp.concatenate([v[:, cells - LANES :], middle], axis=1)

    outer = sweep(
        edge(0, adj), edge(1, grad), edge(2, pre), band_edge, shf, 2 * LANES
    )
    psi[0] = jnp.where(lane < 32, pltpu.roll(outer[:, LANES:], CAP, 1), psi[0])
    psi[-1] = jnp.where(head, psi[-1], outer[:, :LANES])
    ends = jnp.where(head, psi[0], psi[-1])
    row = jnp.zeros((NVAR, LANES), jnp.float32)
    which = lax.broadcasted_iota(jnp.int32, (NVAR, LANES), 0)
    for v in range(NVAR):
        row = jnp.where(which == v, pltpu.roll(ends, 16 * v + HALO, 1), row)
    row = jnp.sum(jnp.where(lane // 16 == which, row, 0.0), axis=0, keepdims=True)
    ends_s[...] = row
    ends_r[0] = row
    pl.semaphore_wait(told, X - 1)
    for s in FAR_FIRST:
        back = (Y - s // X) % Y * X + (X - s % X) % X
        send(ends_s, ends_r.at[back], sent, ends_recv, ahead[s])
    for c in range(blocks):
        out_o[:NVAR, c * LANES : (c + 1) * LANES] = psi[c]
    out_o[NVAR:, :] = jnp.zeros((8 - NVAR, cells), jnp.float32)
    zero_o[...] = jnp.zeros_like(zero_o)

    pl.when(jnp.logical_not(waits))(answer_all)

    found = [jnp.zeros((8, LANES), jnp.float32)] * (faces // LANES)

    def look(dy, ref):
        for dx in range(X):
            got = ref[3 * dx : 3 * dx + 3]
            got = jnp.concatenate([got, got, got[:2]], axis=0)
            for c in range(faces // LANES):
                part = slice(c * LANES, (c + 1) * LANES)
                found[c] = jnp.where(
                    far8[:, part] == dy * X + dx, take_lanes(got, pick[:, part]), found[c]
                )

    look(0, resp_own)
    wait_all(resp_r, 0, len(NEAR), resp_recv.at[0])
    for dy in NEAR:
        look(dy, resp_r.at[SLOT[dy]])
    loads[6].wait()
    wait_all(resp_r, len(NEAR), len(FAR), resp_recv.at[1])
    for dy in FAR:
        look(dy, resp_r.at[SLOT[dy]])
    face_psi = jnp.concatenate(found, axis=1)

    wait_all(ends_r, 1, dom_count - 1, ends_recv)
    ends = ends_r[...].reshape(dom_count, LANES)
    coarse = ends.astype(jnp.bfloat16)
    fine = (ends - coarse.astype(jnp.float32)).astype(jnp.bfloat16)
    picked = lax.dot_general(
        jnp.concatenate([coarse, fine], axis=0),
        jnp.concatenate([reads_b, reads_b], axis=0),
        (((0,), (0,)), ((), ())),
        preferred_element_type=jnp.float32,
    )
    sums = jnp.zeros((2 * dom_count, SENS), jnp.float32)
    for v in range(NVAR):
        end = jnp.where(takes_end, picked[16 * v : 16 * v + 16], 0.0)
        end = jnp.sum(end, axis=0, keepdims=True)
        value = jnp.where(reads_end, end, face_psi[v : v + 1])
        coarse = value.astype(jnp.bfloat16).astype(jnp.float32)
        fine = value - coarse
        weights = jnp.concatenate(
            [jnp.where(feeds, coarse, 0.0), jnp.where(feeds, fine, 0.0)], axis=0
        ).astype(jnp.bfloat16)
        sums = sums + jnp.dot(
            weights,
            jac_v[:, v * SENS : (v + 1) * SENS],
            preferred_element_type=jnp.float32,
        )
    sums = sums[:dom_count] + sums[dom_count:]
    for s in range(1, dom_count):
        part_s[s] = sums[s : s + 1]
    part_r[0] = sums[0:1]
    for s in FAR_FIRST:
        send(part_s.at[s], part_r.at[s], sent, part_recv, ahead[s])
    wait_all(part_r, 1, dom_count - 1, part_recv)
    out_o[NVAR : NVAR + 1, :SENS] = jnp.sum(part_r[...], axis=0)
    wait_all(resp_s, 0, Y - 1, resp_send)
    left_rows = X * (Y - 1) + (X - 1) * 8 * tiles + 2 * (dom_count - 1)
    one_halo = jnp.logical_or(first, last)
    pl.when(one_halo)(lambda: wait_all(count_v, 0, left_rows + 24, sent))
    pl.when(jnp.logical_not(one_halo))(lambda: wait_all(count_v, 0, left_rows + 48, sent))


def solution(mesh):
    groups = mesh.shape["group"]

    def shards(adjoint, gradient, precond, band, face_jac, face_cell, face_box):
        cells = adjoint.shape[1]
        faces = face_jac.shape[0]
        dom_count = X * Y
        packed = cells * NVAR // 8
        f32 = jnp.float32
        vmem = pltpu.VMEM
        dma = pltpu.SemaphoreType.DMA
        out, zero = pl.pallas_call(
            functools.partial(kernel, groups),
            out_shape=(vmem((8, cells), f32), vmem((1, cells), f32)),
            in_specs=[pl.BlockSpec(memory_space=pl.ANY)] * 7,
            out_specs=[pl.BlockSpec(memory_space=pltpu.VMEM)] * 2,
            scratch_shapes=[
                vmem((3, NVAR, cells), f32),
                vmem((BAND, NVAR, NVAR, cells), jnp.bfloat16),
                vmem((faces, NVAR * SENS), jnp.bfloat16),
                vmem((2, 1, faces), jnp.int32),
                vmem((BAND * NVAR, NVAR, cells), f32),
                vmem((BAND * NVAR, NVAR, 2 * LANES), f32),
                vmem((BAND, NVAR, cells), f32),
                vmem((3, 8, LANES), f32),
                vmem((3, 8, LANES), f32),
                vmem((3, 8, LANES), f32),
                vmem((8, packed), f32),
                vmem((X, 8, packed), f32),
                vmem((Y - 1, X, LANES), jnp.int32),
                vmem((Y - 1, X, LANES), jnp.int32),
                vmem((X, LANES), jnp.int32),
                vmem((Y - 1, 3 * X, LANES), f32),
                vmem((Y - 1, 3 * X, LANES), f32),
                vmem((3 * X, LANES), f32),
                vmem((1, LANES), f32),
                vmem((dom_count, 1, LANES), f32),
                vmem((dom_count, 1, LANES), f32),
                vmem((dom_count, 1, LANES), f32),
                vmem((X * (Y - 1) + 3 * packed * 8 // LANES + 2 * dom_count + 46, 1, LANES), f32),
                dma((4,)),
                dma,
                dma((2,)),
                pltpu.SemaphoreType.REGULAR,
                dma,
                dma,
                dma,
                dma((2,)),
                dma,
                dma,
            ],
            compiler_params=pltpu.CompilerParams(
                collective_id=0, has_side_effects=True
            ),
        )(
            adjoint,
            gradient,
            precond,
            band,
            face_jac,
            face_cell.reshape(1, faces),
            face_box.reshape(1, faces),
        )
        state = lax.optimization_barrier(out[:NVAR] + zero)
        zero = zero[:, :SENS] * state[:1, :SENS]
        return state, out[NVAR : NVAR + 1, :SENS] + zero

    return jax.shard_map(
        shards,
        mesh=mesh,
        in_specs=(
            P(None, ("group", "dom")),
            P(None, ("group", "dom")),
            P(None, ("group", "dom")),
            P(None, None, None, ("group", "dom")),
            P(("group", "dom"), None),
            P(("group", "dom")),
            P(("group", "dom"), None),
        ),
        out_specs=(P(None, ("group", "dom")), P(("group", "dom"), None)),
        check_vma=False,
    )
```

```python
import functools

import jax
import jax.numpy as jnp
from jax import lax
from jax.experimental import pallas as pl
from jax.experimental.pallas import tpu as pltpu
from jax.sharding import PartitionSpec as P

NVAR = 6
SENS = 128
BAND = 5
SWEEPS = 3
CAP = 64
HALO = 2 * SWEEPS
LANES = 128
X, Y = 4, 8
MESH = pl.DeviceIdType.MESH

FAR_FIRST = sorted(
    range(1, X * Y),
    key=lambda s: -(min(s % X, X - s % X) + min(s // X, Y - s // X)),
)
NEAR, FAR = (6, 7, 1, 2), (3, 4, 5)
SLOT = {dy: i for i, dy in enumerate(NEAR + FAR)}


def take_lanes(values, index):
    return jnp.take_along_axis(values, index, axis=1, mode="promise_in_bounds")


def sweep(psi, grad, pre, band_ref, shifted_ref, width):
    for _ in range(SWEEPS):
        for k in range(BAND):
            shifted_ref[k, :, :width] = (
                psi if k == 2 else pltpu.roll(psi, (2 - k) % width, 1)
            )
        sums = []
        for k in range(BAND):
            part = None
            for b in range(NVAR):
                column = jnp.broadcast_to(
                    shifted_ref[k, b : b + 1, :width], (NVAR, width)
                )
                term = band_ref[k * NVAR + b] * column
                part = term if part is None else part + term
            sums.append(part)
        total = (sums[0] + sums[1]) + (sums[2] + sums[3]) + sums[4]
        psi = psi + pre * (grad - total)
    return psi


def kernel(
    groups,
    adj_h,
    grad_h,
    pre_h,
    band_h,
    jac_h,
    cell_h,
    box_h,
    out_o,
    zero_o,
    state_v,
    band_v,
    jac_v,
    face_v,
    bandf,
    band_edge,
    shf,
    halo_s,
    halo_l,
    halo_r,
    psi_s,
    psi_r,
    req_s,
    req_r,
    req_own,
    resp_s,
    resp_r,
    resp_own,
    ends_s,
    ends_r,
    part_s,
    part_r,
    count_v,
    in_sem,
    sent,
    halo_recv,
    told,
    psi_recv,
    req_recv,
    resp_send,
    resp_recv,
    ends_recv,
    part_recv,
):
    cells = adj_h.shape[1]
    faces = jac_h.shape[0]
    dom_count = X * Y
    blocks = cells // LANES
    tiles = blocks * NVAR // 8
    g = lax.axis_index("group")
    d = lax.axis_index("dom")
    y, x = d // X, d % X
    rows = [((y + dy) % Y) * X for dy in range(Y)]
    columns = [(x + dx) % X for dx in range(X)]
    ahead = [rows[s // X] + columns[s % X] for s in range(dom_count)]
    total = groups * dom_count
    place = g * dom_count + d
    after = (place + 1) % total
    before = (place + total - 1) % total
    after_id = (after // dom_count, after % dom_count)
    before_id = (before // dom_count, before % dom_count)
    first, last = place == 0, place == total - 1

    loads = [
        pltpu.make_async_copy(src, dst, in_sem.at[i])
        for src, dst, i in (
            (band_h, band_v, 0),
            (adj_h, state_v.at[0], 1),
            (grad_h, state_v.at[1], 1),
            (pre_h, state_v.at[2], 1),
            (cell_h, face_v.at[0], 2),
            (box_h, face_v.at[1], 2),
            (jac_h, jac_v, 3),
        )
    ]
    for load in loads:
        load.start()

    barrier = pltpu.get_barrier_semaphore()

    def greet(target):
        pl.semaphore_signal(barrier, inc=1, device_id=target, device_id_type=MESH)

    lines = [X * dy for dy in (4, 3, 5, 2, 6, 1, 7)] + [2, 1, 3]
    for s in lines:
        greet((g, ahead[s]))
    pl.when(jnp.logical_not(first))(lambda: greet(before_id))
    pl.when(jnp.logical_not(last))(lambda: greet(after_id))

    lane = lax.broadcasted_iota(jnp.int32, (NVAR, LANES), 1)
    head = lane < CAP
    half = BAND * NVAR // 2
    packed = [jnp.zeros((NVAR, LANES), jnp.float32)] * 2
    loads[0].wait()
    for t in range(BAND * NVAR):
        tile = band_v[t // NVAR, t % NVAR].astype(jnp.float32)
        bandf[t] = tile
        start, end = tile[:, :LANES], tile[:, cells - LANES :]
        turned = pltpu.roll(jnp.where(head, start, end), CAP, 1)
        band_edge[t, :, :LANES] = end
        band_edge[t, :, LANES:] = turned
        u = t % half
        ends = jnp.where(lane < 32, start, turned)
        ends = pltpu.roll(ends, 4 * u, 1) if u else ends
        own_lanes = (lane // 4 == u) | (lane // 4 == half + u)
        packed[t // half] = jnp.where(own_lanes, ends, packed[t // half])
    rest = jnp.zeros((8 - NVAR, LANES), jnp.float32)
    halo_s[0] = jnp.concatenate([packed[0], rest], axis=0)
    halo_s[1] = jnp.concatenate([packed[1], rest], axis=0)
    pltpu.make_async_copy(state_v, state_v, in_sem.at[1]).wait()
    adj, grad, pre = state_v[0], state_v[1], state_v[2]
    turned = [
        pltpu.roll(jnp.where(head, v[:, :LANES], v[:, cells - LANES :]), CAP, 1)
        for v in (adj, grad, pre)
    ]
    ends = [
        jnp.where(lane < 32, v[:, :LANES], t) for v, t in zip((adj, grad, pre), turned)
    ]
    packed = jnp.where(
        (lane < 16) | ((lane >= 48) & (lane < 72)),
        ends[0],
        jnp.where(
            (lane < 32) | ((lane >= 72) & (lane < 88)),
            pltpu.roll(ends[1], 16, 1),
            pltpu.roll(ends[2], 32, 1),
        ),
    )
    halo_s[2] = jnp.concatenate([packed, rest], axis=0)

    @pl.when(first)
    def _():
        halo_l[...] = jnp.zeros_like(halo_l)

    @pl.when(last)
    def _():
        halo_r[...] = jnp.zeros_like(halo_r)

    pltpu.make_async_copy(face_v, face_v, in_sem.at[2]).wait()
    cell = face_v[0]
    owner, local = cell // cells, cell % cells
    far = ((owner // X - y + Y) % Y) * X + (owner % X - x + X) % X
    slots = lax.broadcasted_iota(jnp.int32, (dom_count, faces), 0)
    reads = jnp.where(slots == far, 1.0, 0.0)
    earlier = lax.broadcasted_iota(jnp.int32, (faces, faces), 0)
    later = lax.broadcasted_iota(jnp.int32, (faces, faces), 1)
    upper = jnp.where(earlier < later, 1.0, 0.0).astype(jnp.bfloat16)
    reads_b = reads.astype(jnp.bfloat16)
    counts = jnp.dot(reads_b, upper, preferred_element_type=jnp.float32)
    rank = jnp.sum(reads * counts, axis=0, keepdims=True).astype(jnp.int32)
    entry = lax.broadcasted_iota(jnp.int32, (2 * CAP, faces), 0)
    wanted = jnp.where(
        entry < CAP, (local // LANES).astype(jnp.float32), (local % LANES).astype(jnp.float32)
    )
    wanted = jnp.where(entry % CAP == rank, wanted, 0.0).astype(jnp.bfloat16)
    requests = lax.dot_general(
        reads_b, wanted, (((1,), (1,)), ((), ())), preferred_element_type=jnp.float32
    ).astype(jnp.int32)
    req_own[...] = requests[:X]
    for dy in range(1, Y):
        req_s[SLOT[dy]] = requests[X * dy : X * dy + X]

    def send(source, landing, send_sem, recv_sem, target):
        pltpu.make_async_remote_copy(
            src_ref=source,
            dst_ref=landing,
            send_sem=send_sem,
            recv_sem=recv_sem,
            device_id=(g, target),
            device_id_type=MESH,
        ).start()

    def wait_all(ref, start, count, sem):
        some = ref.at[pl.ds(start, count)]
        pltpu.make_async_copy(some, some, sem).wait()

    inner = sweep(adj, grad, pre, bandf, shf, cells)
    psi = [inner[:, c * LANES : (c + 1) * LANES] for c in range(blocks)]
    spare = jnp.concatenate(psi[tiles:], axis=0)
    for c in range(tiles):
        part = slice(c * LANES, (c + 1) * LANES)
        psi_s[:, part] = jnp.concatenate([psi[c], spare[2 * c : 2 * c + 2]], axis=0)

    missing = first.astype(jnp.int32) + last.astype(jnp.int32)
    pl.semaphore_wait(barrier, len(lines) + 2 - missing)

    halo_copies = []
    for i, (target, landing) in enumerate(((after_id, halo_l), (before_id, halo_r))):
        halo_copies.append(
            pltpu.make_async_remote_copy(
                src_ref=halo_s,
                dst_ref=landing,
                send_sem=sent,
                recv_sem=halo_recv.at[i],
                device_id=target,
                device_id_type=MESH,
            )
        )
    pl.when(jnp.logical_not(last))(halo_copies[0].start)
    pl.when(jnp.logical_not(first))(halo_copies[1].start)

    for dy in (4, 3, 5, 2, 6, 1, 7):
        i = SLOT[dy]
        send(req_s.at[i], req_r.at[i], sent, req_recv, ahead[X * dy])
    for dx in (2, 1, 3):
        i = X - dx
        send(psi_s, psi_r.at[i], sent, psi_recv, ahead[dx])
    for dx in (2, 1, 3):
        pl.semaphore_signal(
            told, inc=1, device_id=(g, ahead[dx]), device_id_type=MESH
        )

    pick = jnp.broadcast_to(rank, (8, faces)) + jnp.where(
        lax.broadcasted_iota(jnp.int32, (8, faces), 0) < 3, 0, CAP
    )
    far8 = jnp.broadcast_to(far, (8, faces))
    box = face_v[1]
    box_far = ((box // X - y + Y) % Y) * X + (box % X - x + X) % X
    feeds = slots == box_far
    at_start, at_end = local < HALO, local >= cells - HALO
    end_place = jnp.where(at_start, local + HALO, local - (cells - HALO))
    takes_end = lax.broadcasted_iota(jnp.int32, (16, faces), 0) == end_place
    reads_end = at_start | at_end

    low8 = lax.broadcasted_iota(jnp.int32, (8, LANES), 1) < CAP
    low1 = low8[:1]

    def row_values(ref):
        parts = [ref[:, c * LANES : (c + 1) * LANES] for c in range(tiles)]
        size = 8 - NVAR
        for start in range(0, tiles, NVAR // size):
            some = [p[NVAR:] for p in parts[start : start + NVAR // size]]
            parts.append(jnp.concatenate(some + some[:1], axis=0))
        return parts

    def answers(values, wish, other):
        chunk = jnp.where(low1, wish, pltpu.roll(other, CAP, 1))
        place_in = jnp.where(low1, pltpu.roll(wish, CAP, 1), other)
        chunk = jnp.broadcast_to(chunk, (8, LANES))
        place_in = jnp.broadcast_to(place_in, (8, LANES))
        found = take_lanes(values[0], place_in)
        for c in range(1, blocks):
            found = jnp.where(chunk == c, take_lanes(values[c], place_in), found)
        turned = pltpu.roll(found, 5, 0)
        return (
            jnp.where(low8, found, pltpu.roll(turned, CAP, 1))[:3],
            jnp.where(low8, pltpu.roll(found, CAP, 1), turned)[:3],
        )

    pairs = ((4, 3), (5, 2), (6, 1), (7, 0))

    def answer(values, dx, pair):
        a, b = pair
        wish = req_r[SLOT[a], dx : dx + 1]
        other = req_r[SLOT[b], dx : dx + 1] if b else req_own[dx : dx + 1]
        one, two = answers(values, wish, other)
        resp_s[SLOT[a], 3 * dx : 3 * dx + 3] = one
        if b:
            resp_s[SLOT[b], 3 * dx : 3 * dx + 3] = two
        else:
            resp_own[3 * dx : 3 * dx + 3] = two

    def answer_all():
        wait_all(psi_r, 1, X - 1, psi_recv)
        wait_all(req_r, 0, Y - 1, req_recv)
        values = [row_values(psi_s)] + [row_values(psi_r.at[dx]) for dx in range(1, X)]
        for pair in pairs:
            for dx in range(X):
                answer(values[dx], dx, pair)
            for dy in pair:
                if dy:
                    i = SLOT[dy]
                    send(
                        resp_s.at[i],
                        resp_r.at[i],
                        resp_send,
                        resp_recv.at[0 if dy in NEAR else 1],
                        ahead[X * (Y - dy)],
                    )

    waits = place == (Y // 2) * X - 1
    pl.when(waits)(answer_all)

    pl.when(jnp.logical_not(first))(halo_copies[0].wait_recv)
    pl.when(jnp.logical_not(last))(halo_copies[1].wait_recv)
    left = halo_l[:, :NVAR, :]
    right = halo_r[:, :NVAR, :]
    for h in range(2):
        both = jnp.where(lane < 4 * half, right[h], left[h])
        for u in range(half):
            back = pltpu.roll(both, LANES - 4 * u, 1) if u else both
            band_edge[h * half + u, :, LANES : LANES + CAP] = back[:, :CAP]
    both = jnp.where(lane < 48, right[2], left[2])

    def edge(i, v):
        back = pltpu.roll(both, LANES - 16 * i, 1) if i else both
        middle = jnp.where(head, back, turned[i])
        return jnp.concatenate([v[:, cells - LANES :], middle], axis=1)

    outer = sweep(
        edge(0, adj), edge(1, grad), edge(2, pre), band_edge, shf, 2 * LANES
    )
    psi[0] = jnp.where(lane < 32, pltpu.roll(outer[:, LANES:], CAP, 1), psi[0])
    psi[-1] = jnp.where(head, psi[-1], outer[:, :LANES])
    ends = jnp.where(head, psi[0], psi[-1])
    row = jnp.zeros((NVAR, LANES), jnp.float32)
    which = lax.broadcasted_iota(jnp.int32, (NVAR, LANES), 0)
    for v in range(NVAR):
        row = jnp.where(which == v, pltpu.roll(ends, 16 * v + HALO, 1), row)
    row = jnp.sum(jnp.where(lane // 16 == which, row, 0.0), axis=0, keepdims=True)
    ends_s[...] = row
    ends_r[0] = row
    pl.semaphore_wait(told, X - 1)
    for s in FAR_FIRST:
        back = (Y - s // X) % Y * X + (X - s % X) % X
        send(ends_s, ends_r.at[back], sent, ends_recv, ahead[s])
    for c in range(blocks):
        out_o[:NVAR, c * LANES : (c + 1) * LANES] = psi[c]
    out_o[NVAR:, :] = jnp.zeros((8 - NVAR, cells), jnp.float32)
    zero_o[...] = jnp.zeros_like(zero_o)

    pl.when(jnp.logical_not(waits))(answer_all)

    found = [jnp.zeros((8, LANES), jnp.float32)] * (faces // LANES)

    def look(dy, ref):
        for dx in range(X):
            got = ref[3 * dx : 3 * dx + 3]
            got = jnp.concatenate([got, got, got[:2]], axis=0)
            for c in range(faces // LANES):
                part = slice(c * LANES, (c + 1) * LANES)
                found[c] = jnp.where(
                    far8[:, part] == dy * X + dx, take_lanes(got, pick[:, part]), found[c]
                )

    look(0, resp_own)
    wait_all(resp_r, 0, len(NEAR), resp_recv.at[0])
    for dy in NEAR:
        look(dy, resp_r.at[SLOT[dy]])
    loads[6].wait()
    wait_all(resp_r, len(NEAR), len(FAR), resp_recv.at[1])
    for dy in FAR:
        look(dy, resp_r.at[SLOT[dy]])
    face_psi = jnp.concatenate(found, axis=1)

    wait_all(ends_r, 1, dom_count - 1, ends_recv)
    ends = ends_r[...].reshape(dom_count, LANES)
    coarse = ends.astype(jnp.bfloat16)
    fine = (ends - coarse.astype(jnp.float32)).astype(jnp.bfloat16)
    picked = lax.dot_general(
        jnp.concatenate([coarse, fine], axis=0),
        jnp.concatenate([reads_b, reads_b], axis=0),
        (((0,), (0,)), ((), ())),
        preferred_element_type=jnp.float32,
    )
    sums = jnp.zeros((2 * dom_count, SENS), jnp.float32)
    for v in range(NVAR):
        end = jnp.where(takes_end, picked[16 * v : 16 * v + 16], 0.0)
        end = jnp.sum(end, axis=0, keepdims=True)
        value = jnp.where(reads_end, end, face_psi[v : v + 1])
        coarse = value.astype(jnp.bfloat16).astype(jnp.float32)
        fine = value - coarse
        weights = jnp.concatenate(
            [jnp.where(feeds, coarse, 0.0), jnp.where(feeds, fine, 0.0)], axis=0
        ).astype(jnp.bfloat16)
        sums = sums + jnp.dot(
            weights,
            jac_v[:, v * SENS : (v + 1) * SENS],
            preferred_element_type=jnp.float32,
        )
    sums = sums[:dom_count] + sums[dom_count:]
    for s in range(1, dom_count):
        part_s[s] = sums[s : s + 1]
    part_r[0] = sums[0:1]
    for s in FAR_FIRST:
        send(part_s.at[s], part_r.at[s], sent, part_recv, ahead[s])
    wait_all(part_r, 1, dom_count - 1, part_recv)
    out_o[NVAR : NVAR + 1, :SENS] = jnp.sum(part_r[...], axis=0)
    wait_all(resp_s, 0, Y - 1, resp_send)
    left_rows = X * (Y - 1) + (X - 1) * 8 * tiles + 2 * (dom_count - 1)
    one_halo = jnp.logical_or(first, last)
    pl.when(one_halo)(lambda: wait_all(count_v, 0, left_rows + 24, sent))
    pl.when(jnp.logical_not(one_halo))(lambda: wait_all(count_v, 0, left_rows + 48, sent))


def solution(mesh):
    groups = mesh.shape["group"]

    def shards(adjoint, gradient, precond, band, face_jac, face_cell, face_box):
        cells = adjoint.shape[1]
        faces = face_jac.shape[0]
        dom_count = X * Y
        packed = cells * NVAR // 8
        f32 = jnp.float32
        vmem = pltpu.VMEM
        dma = pltpu.SemaphoreType.DMA
        out, zero = pl.pallas_call(
            functools.partial(kernel, groups),
            out_shape=(vmem((8, cells), f32), vmem((1, cells), f32)),
            in_specs=[pl.BlockSpec(memory_space=pl.ANY)] * 7,
            out_specs=[pl.BlockSpec(memory_space=pltpu.VMEM)] * 2,
            scratch_shapes=[
                vmem((3, NVAR, cells), f32),
                vmem((BAND, NVAR, NVAR, cells), jnp.bfloat16),
                vmem((faces, NVAR * SENS), jnp.bfloat16),
                vmem((2, 1, faces), jnp.int32),
                vmem((BAND * NVAR, NVAR, cells), f32),
                vmem((BAND * NVAR, NVAR, 2 * LANES), f32),
                vmem((BAND, NVAR, cells), f32),
                vmem((3, 8, LANES), f32),
                vmem((3, 8, LANES), f32),
                vmem((3, 8, LANES), f32),
                vmem((8, packed), f32),
                vmem((X, 8, packed), f32),
                vmem((Y - 1, X, LANES), jnp.int32),
                vmem((Y - 1, X, LANES), jnp.int32),
                vmem((X, LANES), jnp.int32),
                vmem((Y - 1, 3 * X, LANES), f32),
                vmem((Y - 1, 3 * X, LANES), f32),
                vmem((3 * X, LANES), f32),
                vmem((1, LANES), f32),
                vmem((dom_count, 1, LANES), f32),
                vmem((dom_count, 1, LANES), f32),
                vmem((dom_count, 1, LANES), f32),
                vmem((X * (Y - 1) + 3 * packed * 8 // LANES + 2 * dom_count + 46, 1, LANES), f32),
                dma((4,)),
                dma,
                dma((2,)),
                pltpu.SemaphoreType.REGULAR,
                dma,
                dma,
                dma,
                dma((2,)),
                dma,
                dma,
            ],
            compiler_params=pltpu.CompilerParams(
                collective_id=0, has_side_effects=True
            ),
        )(
            adjoint,
            gradient,
            precond,
            band,
            face_jac,
            face_cell.reshape(1, faces),
            face_box.reshape(1, faces),
        )
        state = lax.optimization_barrier(out[:NVAR] + zero)
        zero = zero[:, :SENS] * state[:1, :SENS]
        return state, out[NVAR : NVAR + 1, :SENS] + zero

    return jax.shard_map(
        shards,
        mesh=mesh,
        in_specs=(
            P(None, ("group", "dom")),
            P(None, ("group", "dom")),
            P(None, ("group", "dom")),
            P(None, None, None, ("group", "dom")),
            P(("group", "dom"), None),
            P(("group", "dom")),
            P(("group", "dom"), None),
        ),
        out_specs=(P(None, ("group", "dom")), P(("group", "dom"), None)),
        check_vma=False,
    )
```
